32 devices in a mesh: grp: 4 (over y, core), dev: 8 (over z, x).
Axes of the slice: x: 2, y: 2, z: 4, core: 2. Of those that a mesh axis runs over, the one named last changes fastest.
Arguments:
- matrix: float32 [16384, 128], P(('grp', 'dev')), may hold values from -6 to 6
- flip_bits: int32 [16384], P(('grp', 'dev')), may hold values from 0 to 1
- sample_rows: int32 [2048], replicated, may hold values from 0 to 16383
Outputs:
- sketch: float32 [2048, 128], P(('grp', 'dev'))
- gram: float32 [128, 128], replicated
The draws below stay inside these ranges and needn't reach their ends.
Inputs may be any that keep to these rules, and one draw needn't show every extreme that they name: `sample_rows`: rows may repeat.
All inputs are finite; a program needn't handle non-finite values.
Results may differ from the reference program's by a relative error of at most 0.000098.
Values sent between devices are 32-bit elements; how exact they have to be, the bound alone decides.
A program may use at most 64 MiB of HBM per device.

```python
import jax
import jax.numpy as jnp
from jax import lax

F = 128
SAMPLES = 2048
ROWS = 16384


def plant(result, own_key, low, largest):
    shape = result.shape
    spot = [jax.random.randint(jax.random.fold_in(own_key, axis), (), 0, shape[axis]) for axis in range(len(shape))]
    result = result.at[tuple(spot)].set(low)
    longest = shape.index(max(shape))
    spot[longest] = (spot[longest] + 1) % shape[longest]
    return result.at[tuple(spot)].set(largest)


def block_levels(key, extent, shards, smallest, high):
    level = 1.0
    for axis_at, shards_of in shards:
        heights = jax.random.uniform(jax.random.fold_in(jax.random.fold_in(key, 6), axis_at), (shards_of,), jnp.float32, smallest / len(shards), high / len(shards))
        level = level * jnp.repeat(jnp.exp(heights), extent[axis_at] // shards_of).reshape((-1,) + (1,) * (len(extent) - 1 - axis_at))
    return level


def gaussian(stream_key, extent, scale, reach, shards=(), held_as=jnp.bfloat16):
    entries = jax.random.normal(stream_key, extent, jnp.float32) * scale
    if len(shards) > 0:
        entries = block_levels(stream_key, extent, shards, -0.22, 0.18) * entries
    return jnp.clip(entries, min=-reach, max=reach).astype(held_as)


def setup_inputs(seed: int = 0) -> dict:
    seeds = jax.random.split(jax.random.key(seed), 4)
    return {
        "matrix": gaussian(seeds[0], (ROWS, F), 1.0, 6.0, ((0, 32),), jnp.float32),
        "flip_bits": plant(jax.random.randint(seeds[1], (ROWS,), 0, 2), jax.random.fold_in(seeds[1], 1), 0, 1).astype(jnp.int32),
        "sample_rows": plant(jax.random.randint(seeds[2], (SAMPLES,), 0, ROWS), jax.random.fold_in(seeds[2], 1), 0, ROWS - 1).astype(jnp.int32),
    }


def reference(matrix, flip_bits, sample_rows):
    signs = (1 - 2 * flip_bits).astype(jnp.float32)
    mixed = matrix * signs[:, None]
    width = matrix.shape[1]
    half = 1
    for level in range(ROWS.bit_length() - 1):
        cube = mixed.reshape(-1, 2, half, width)
        first = cube[:, 0]
        second = cube[:, 1]
        mixed = jnp.stack([first + second, first - second], axis=1).reshape(ROWS, width)
        half = half * 2
    mixed = mixed / jnp.sqrt(jnp.float32(ROWS))
    sketch = jnp.take(mixed, sample_rows, axis=0)
    gram = jnp.dot(sketch.T, sketch, preferred_element_type=jnp.float32, precision=lax.Precision.HIGHEST) / SAMPLES
    return (sketch, gram)
```

```python
import functools
import math

import jax
import jax.numpy as jnp
from jax import lax
from jax.experimental import pallas as pl
from jax.experimental.pallas import tpu as pltpu
from jax.sharding import PartitionSpec as P

MESH = pl.DeviceIdType.MESH
LANES = 128


def loop(count, fn):
    if count <= 8:
        for step in range(count):
            fn(step)
    else:
        lax.fori_loop(0, count, lambda step, carry: (fn(step), carry)[1], 0)


def parity(bits, width):
    shift = 1
    while shift * 2 < width:
        shift *= 2
    while shift:
        bits = bits ^ (bits >> shift)
        shift //= 2
    return bits & 1


def sign_of(bits, width):
    return (1 - 2 * parity(bits, width)).astype(jnp.float32)


def split3(value):
    high = value.astype(jnp.bfloat16)
    rest = value - high.astype(jnp.float32)
    mid = rest.astype(jnp.bfloat16)
    low = (rest - mid.astype(jnp.float32)).astype(jnp.bfloat16)
    return high, mid, low


def kernel(
    n_grp, n_dev, rows, own,
    x_ref, flip_hbm, sample_hbm, sketch_ref, gram_ref,
    flip_ref, sample_ref, x_full, slabs, flips, cols, index, base, part, blocks, gpart, gslots, gfull, reduced,
    load_sem, pair_send, pair_recv, twin_send, twin_recv, fwd_send, fwd_recv,
    flip_send, flip_recv, rs_send, rs_recv, g_send, g_recv, b_send, b_recv,
    ready,
):
    f32 = jnp.float32
    devices = n_grp * n_dev
    n_y, n_z = n_grp // 2, n_dev // 2
    groups = n_y * n_z
    width = x_ref.shape[1]
    pieces = twin_send.shape[0]
    piece = rows // pieces
    samples = sample_hbm.shape[0] * LANES
    row_bits = rows.bit_length() - 1
    all_bits = (rows * devices).bit_length() - 1
    me_g, me_d = lax.axis_index("grp"), lax.axis_index("dev")
    core, y = lax.rem(me_g, 2), lax.div(me_g, 2)
    x, z = lax.rem(me_d, 2), lax.div(me_d, 2)
    pair_g = me_g + 1 - 2 * core
    twin_d = me_d + 1 - 2 * x
    mine = y * n_z + z

    def remote(src, dst, send, recv, grp, dev):
        return pltpu.make_async_remote_copy(
            src_ref=src, dst_ref=dst, send_sem=send, recv_sem=recv,
            device_id=(grp, dev), device_id_type=MESH,
        )

    barrier = pltpu.get_barrier_semaphore()

    def signal(sem, grp, dev):
        pl.semaphore_signal(sem, inc=1, device_id=(grp, dev), device_id_type=MESH)

    def along_y(step):
        return me_g + 2 * step, me_d

    def along_z(step):
        return me_g, me_d + 2 * step

    def tell_line(sem, at, size, reach, along):
        for step in range(1, min(reach, size - 1) + 1):
            @pl.when(at >= step)
            def _():
                signal(sem, *along(-step))

            @pl.when(at + step < size)
            def _():
                signal(sem, *along(step))

    def line_count(at, size, reach):
        return jnp.minimum(at, reach) + jnp.minimum(size - 1 - at, reach)

    signal(barrier, pair_g, me_d)
    signal(barrier, me_g, twin_d)
    tell_line(barrier, y, n_y, 1, along_y)
    tell_line(barrier, z, n_z, 1, along_z)

    loads = [
        pltpu.make_async_copy(sample_hbm, sample_ref, load_sem.at[0]),
        pltpu.make_async_copy(flip_hbm, flip_ref, load_sem.at[1]),
        pltpu.make_async_copy(x_ref, x_full, load_sem.at[2]),
    ]
    for copy in loads:
        copy.start()
    pl.semaphore_wait(barrier, 2 + line_count(y, n_y, 1) + line_count(z, n_z, 1))

    rounds = []
    for at, size, along in ((z, n_z, along_z), (y, n_y, along_y)):
        reach = 1
        while reach < size - 1:
            rounds.append((at, size, reach, along))
            reach *= 2
    rounds.append((y, n_y, n_y - 1, along_y))

    def open_round(k):
        if k < len(rounds):
            at, size, reach, along = rounds[k]
            tell_line(ready.at[k], at, size, reach, along)
        elif k == len(rounds):
            signal(ready.at[k], me_g, twin_d)
        else:
            signal(ready.at[k], pair_g, me_d)

    def close_round(k):
        if k < len(rounds):
            at, size, reach, along = rounds[k]
            pl.semaphore_wait(ready.at[k], line_count(at, size, reach))
        else:
            pl.semaphore_wait(ready.at[k], 1)

    half = width // 2
    left = lax.broadcasted_iota(jnp.int32, (1, width), 1) < half

    def swap(value):
        return pltpu.roll(value, half, value.ndim - 1)

    for copy in loads:
        copy.wait()
    top, bottom = x_full[pl.ds(0, rows // 2), :], x_full[pl.ds(rows // 2, rows // 2), :]
    slabs[0, 0] = jnp.where(left, top, swap(bottom))
    slabs[1, 0] = jnp.where(left, swap(top), bottom)
    twin, pair = [], []
    for h in range(2):
        for c in range(pieces // 2):
            at = pl.ds(c * piece, piece)
            k = h * (pieces // 2) + c
            copy = remote(
                slabs.at[h, 0, at], slabs.at[h, 2, at],
                twin_send.at[k], twin_recv.at[k], me_g, twin_d,
            )
            copy.start()
            twin.append(copy)
    for h in range(2):
        copy = remote(
            slabs.at[h, 0], slabs.at[h, 1], pair_send.at[h], pair_recv.at[h], pair_g, me_d
        )
        copy.start()
        pair.append(copy)
    flip_copies = [
        remote(flip_ref, flips.at[0], flip_send.at[0], flip_recv.at[0], pair_g, me_d),
        remote(flip_ref, flips.at[1], flip_send.at[1], flip_recv.at[1], me_g, twin_d),
        remote(flips.at[1], flips.at[2], flip_send.at[2], flip_recv.at[2], pair_g, me_d),
    ]
    open_round(0)
    for copy in flip_copies[:2]:
        copy.start()

    span = n_dev * own // LANES
    for i in range(n_y):
        for r in range(span):
            line = sample_ref[pl.ds((i * 2 + core) * span + r, 1), :]
            cols[pl.ds((i * span + r) * LANES, LANES), :] = jnp.transpose(
                jnp.broadcast_to(line, (LANES, LANES))
            )
    for i in range(n_y):
        for j in range(n_z):
            index[pl.ds((i * n_z + j) * own, own), :] = cols[
                pl.ds((i * n_dev + j * 2 + x) * own, own), :
            ]
    close_round(0)
    open_round(1)
    picks = groups * own
    wanted = index[...]
    for k in range(rows // LANES):
        lane = lax.broadcasted_iota(jnp.int32, (picks, LANES), 1) + k * LANES
        base[:, k * LANES:(k + 1) * LANES] = sign_of(wanted & lane, row_bits).astype(jnp.bfloat16)

    owner_signs = [
        sign_of(wanted & ((grp * n_dev + dev) * rows), all_bits)
        for grp, dev in ((me_g, me_d), (pair_g, me_d), (me_g, twin_d), (pair_g, twin_d))
    ]

    def term(h, slot, flip_bits, grp, dev):
        signs = base[...]
        toggles = (1 - 2 * flip_bits).astype(f32).astype(jnp.bfloat16)
        signs = jnp.concatenate(
            [
                signs[:, k * LANES:(k + 1) * LANES] * toggles[k:k + 1, :]
                for k in range(rows // LANES)
            ],
            axis=1,
        )
        packed = slabs[h, slot]
        high, mid, low = split3(packed)
        high_s, mid_s, low_s = split3(swap(packed))
        right = jnp.concatenate(
            [
                jnp.concatenate([jnp.where(left, high, mid_s), low], axis=1),
                jnp.concatenate([jnp.where(left, high_s, mid), low_s], axis=1),
            ],
            axis=0,
        )
        product = jnp.dot(signs, right, preferred_element_type=f32)
        first, last = product[:, :width], product[:, width:]
        return (first + swap(first) + last) * owner_signs[slot]

    def give(h, i, j):
        to_y, to_z = lax.rem(y + i, n_y), lax.rem(z + j, n_z)
        remote(
            part.at[h, to_y * n_z + to_z], blocks.at[h, mine], rs_send.at[h], rs_recv.at[h],
            to_y * 2 + core, to_z * 2 + x,
        ).start()

    for k in range(1, len(rounds) - 1):
        close_round(k)
        open_round(k + 1)
    totals = [term(h, 0, flip_ref[...], me_g, me_d) for h in range(2)]
    close_round(len(rounds) - 1)
    open_round(len(rounds))
    flip_copies[0].wait_recv()
    for h in range(2):
        pair[h].wait_recv()
        totals[h] = totals[h] + term(h, 1, flips[0], pair_g, me_d)
    flip_copies[1].wait_recv()
    flip_copies[2].start()
    forward = []
    for h in range(2):
        for c in range(pieces // 2):
            at = pl.ds(c * piece, piece)
            k = h * (pieces // 2) + c
            twin[k].wait_recv()
            copy = remote(
                slabs.at[h, 2, at], slabs.at[h, 3, at],
                fwd_send.at[k], fwd_recv.at[k], pair_g, me_d,
            )
            copy.start()
            forward.append(copy)
        total = totals[h] + term(h, 2, flips[1], me_g, twin_d)
        if h == 0:
            flip_copies[2].wait_recv()
        for copy in forward[h * (pieces // 2):]:
            copy.wait_recv()
        total = total + term(h, 3, flips[2], pair_g, twin_d)
        total = total.reshape(groups, own, width)
        part[h] = jnp.where(
            left.reshape(1, 1, width), total[:, :own // 2], swap(total[:, own // 2:])
        )
        if h == 0:
            close_round(len(rounds))
            open_round(len(rounds) + 1)
        for i in range(n_y - 1, -1, -1):
            loop(n_z - (i == 0), lambda j: give(h, i, j + (i == 0)))
        blocks[h, mine] = part[h, mine]
    sums = []
    for h in range(2):
        others = blocks.at[h, pl.ds(0, groups - 1)]
        pltpu.make_async_copy(others, others, rs_recv.at[h]).wait()
        summed = blocks[h, 0]
        for i in range(1, groups):
            summed = summed + blocks[h, i]
        sums.append(summed)
    sketch = jnp.concatenate(
        [
            jnp.where(left, sums[0], swap(sums[1])),
            jnp.where(left, swap(sums[0]), sums[1]),
        ],
        axis=0,
    )
    sketch = sketch * (1.0 / math.sqrt(rows * devices))
    sketch_ref[...] = sketch

    close_round(len(rounds) + 1)
    chunks = gfull.shape[0]
    across = min(chunks, n_dev // 2)
    first = (n_dev - across) // 2
    chunk = width // chunks
    linear = me_g * n_dev + me_d
    reducer = (me_g < chunks // across) & (me_d >= first) & (me_d < first + across)
    my_chunk = me_g * across + me_d - first
    gram = lax.dot_general(
        sketch, sketch, (((0,), (0,)), ((), ())),
        precision=lax.Precision.HIGHEST, preferred_element_type=f32,
    )
    gpart[...] = gram.reshape(chunks, chunk, width)
    turn = lax.rem(linear, chunks)
    for k in range(chunks):
        to = lax.rem(k + turn, chunks)
        to_g, to_d = lax.div(to, across), first + lax.rem(to, across)

        @pl.when((me_g != to_g) | (me_d != to_d))
        def _():
            remote(gpart.at[to], gslots.at[linear], g_send, g_recv, to_g, to_d).start()

    @pl.when(reducer)
    def _():
        gslots[linear] = gpart[my_chunk]
        rest = gslots.at[pl.ds(0, devices - 1)]
        pltpu.make_async_copy(rest, rest, g_recv).wait()
        result = jnp.sum(gslots[...], axis=0) * (1.0 / samples)
        reduced[...] = result
        gfull[my_chunk] = result

        def tell(i, j):
            remote(
                reduced, gfull.at[my_chunk], b_send, b_recv,
                lax.rem(me_g + i, n_grp), lax.rem(me_d + j, n_dev),
            ).start()

        for i in range(n_grp - 1, -1, -1):
            loop(n_dev - (i == 0), lambda j: tell(i, j + (i == 0)))
        most = gfull.at[pl.ds(0, chunks - 1)]
        pltpu.make_async_copy(most, most, b_recv).wait()
        pltpu.make_async_copy(rest, rest, b_send).wait()
        pltpu.make_async_copy(most, most, g_send).wait()

    @pl.when(jnp.logical_not(reducer))
    def _():
        pltpu.make_async_copy(gfull, gfull, b_recv).wait()
        pltpu.make_async_copy(gfull, gfull, g_send).wait()

    gram_ref[...] = gfull[...].reshape(width, width)
    for copy in twin + forward + flip_copies + pair:
        copy.wait_send()
    for h in range(2):
        others = blocks.at[h, pl.ds(0, groups - 1)]
        pltpu.make_async_copy(others, others, rs_send.at[h]).wait()


def split2(value):
    high = value.astype(jnp.bfloat16)
    return high, (value - high.astype(jnp.float32)).astype(jnp.bfloat16)


def plane_kernel(
    n_grp, n_dev, rows, own,
    x_hbm, flip_hbm, sample_hbm, sketch_ref, gram_ref,
    x_ref, flip_ref, sample_ref, turned, slabs, signs, peer_signs, part, blocks, mixed, cols, turn_back,
    gpart, gslots, ghalf, gmine, gfull,
    load_sem, in_send, in_recv, z_send, z_recv, out_send, out_recv, core_send, core_recv, gz_send, gz_recv,
):
    f32, bf16 = jnp.float32, jnp.bfloat16
    width = x_ref.shape[1]
    n_y, n_z = n_grp // 2, n_dev // 2
    peers = n_grp * 2
    mine = width // peers
    span = n_dev * own // LANES
    samples = sample_ref.shape[0] * LANES
    picks = n_grp * LANES
    row_bits = rows.bit_length() - 1
    all_bits = (rows * n_grp * n_dev).bit_length() - 1
    me_g, me_d = lax.axis_index("grp"), lax.axis_index("dev")
    core, y = lax.rem(me_g, 2), lax.div(me_g, 2)
    x, z = lax.rem(me_d, 2), lax.div(me_d, 2)
    me = me_g * 2 + x

    plane = [(a, k, b) for a in range(n_y) for k in range(2) for b in range(2)][:0:-1]
    plane = sorted(plane, key=lambda at: -((at[0] > 0) + at[1]))

    def peer(a, k, b):
        to_y, to_x, to_c = lax.rem(y + a, n_y), lax.rem(x + k, 2), lax.rem(core + b, 2)
        return to_y * 2 + to_c, to_x, to_c

    def remote(src, dst, send, recv, grp, dev):
        return pltpu.make_async_remote_copy(
            src_ref=src, dst_ref=dst, send_sem=send, recv_sem=recv,
            device_id=(grp, dev), device_id_type=MESH,
        )

    barrier = pltpu.get_barrier_semaphore()
    loads = [
        pltpu.make_async_copy(x_hbm, x_ref, load_sem.at[0]),
        pltpu.make_async_copy(flip_hbm, flip_ref, load_sem.at[1]),
        pltpu.make_async_copy(sample_hbm, sample_ref, load_sem.at[2]),
    ]
    for at in plane:
        grp, to_x, _ = peer(*at)
        pl.semaphore_signal(barrier, inc=1, device_id=(grp, z * 2 + to_x), device_id_type=MESH)
    for d in range(1, n_z):
        pl.semaphore_signal(
            barrier, inc=1, device_id=(me_g, lax.rem(z + d, n_z) * 2 + x), device_id_type=MESH
        )
    for copy in loads:
        copy.start()
    for copy in loads:
        copy.wait()

    toggles = (1 - 2 * flip_ref[...]).astype(f32)
    for k in range(rows // LANES):
        at = slice(k * LANES, (k + 1) * LANES)
        turned[:, at] = jnp.transpose(x_ref[at, :]) * toggles[k:k + 1, :]
    pl.semaphore_wait(barrier, peers - 1 + n_z - 1)

    sent = []
    for m, at in enumerate(plane):
        grp, to_x, _ = peer(*at)
        to = grp * 2 + to_x
        copy = remote(
            turned.at[pl.ds(pl.multiple_of(to * mine, mine), mine)], slabs.at[me],
            in_send.at[m], in_recv.at[m], grp, z * 2 + to_x,
        )
        copy.start()
        sent.append(copy)
    slabs[me] = turned[pl.ds(pl.multiple_of(me * mine, mine), mine), :]

    order = sorted(range(n_z), key=lambda d: -min(d, n_z - d))
    low = lax.broadcasted_iota(jnp.int32, (16, LANES), 0)
    for i, d in enumerate(order):
        to_z = lax.rem(z + d, n_z)
        for g in range(n_grp):
            wanted = sample_ref[pl.ds(g * span + to_z, 1), :]
            wide = jnp.broadcast_to(wanted, (16, LANES))
            pieces = [sign_of(wide & low, 16).astype(bf16)]
            for bit in range(4, row_bits):
                factor = (1 - 2 * ((wide >> bit) & 1)).astype(f32).astype(bf16)
                pieces += [piece * factor for piece in pieces]
            for k, piece in enumerate(pieces):
                signs[i, k * 16:(k + 1) * 16, g * LANES:(g + 1) * LANES] = piece
            wide = wide[:8]
            for p in range(peers):
                holder = ((p // 2) * n_dev + z * 2 + p % 2) * rows
                peer_signs[i, p, :, g * LANES:(g + 1) * LANES] = sign_of(wide & holder, all_bits)

    for copy in sent:
        copy.wait_recv()
    high, mid = split2(slabs[...].reshape(peers * mine, rows))
    left = jnp.concatenate([high, mid], axis=0)
    passed = []
    for i, d in enumerate(order):
        product = jnp.dot(left, signs[i], preferred_element_type=f32)
        product = product[:peers * mine] + product[peers * mine:]
        total = None
        for p in range(peers):
            term = product[p * mine:(p + 1) * mine].reshape(mine // 8, 8, picks) * peer_signs[i, p][None]
            total = term if total is None else total + term
        part[i] = total.reshape(mine, picks)
        if d:
            copy = remote(
                part.at[i], blocks.at[i], z_send.at[i], z_recv.at[i],
                me_g, lax.rem(z + d, n_z) * 2 + x,
            )
            copy.start()
            passed.append(copy)
    total = part[n_z - 1]
    for i, copy in enumerate(passed):
        copy.wait_recv()
        total = total + blocks[i]
    total = total * (1.0 / math.sqrt(rows * n_grp * n_dev))
    for c in range(2):
        mixed[c] = jnp.concatenate(
            [total[:, g * LANES:(g + 1) * LANES] for g in range(c, n_grp, 2)], axis=1
        )
    given = []
    for m, at in enumerate(plane):
        grp, to_x, to_c = peer(*at)
        copy = remote(
            mixed.at[to_c], cols.at[me], out_send.at[m], out_recv.at[m], grp, z * 2 + to_x
        )
        copy.start()
        given.append(copy)
    cols[me] = mixed[core]
    for copy in given:
        copy.wait_recv()

    held = cols[...].reshape(width, n_y * LANES)
    high, mid = split2(held)
    gram = lax.dot_general(
        jnp.concatenate([high, mid, high], axis=1), jnp.concatenate([high, high, mid], axis=1),
        (((1,), (1,)), ((), ())), preferred_element_type=f32,
    )
    half = width // 2
    gpart[...] = (gram * (1.0 / samples)).reshape(2, half, width)
    sibling = me_g + 1 - 2 * core
    swap = remote(gpart.at[1 - core], gslots, core_send.at[0], core_recv.at[0], sibling, me_d)
    swap.start()
    block = cols[:, :, pl.ds(pl.multiple_of(y * LANES, LANES), LANES)].reshape(width, LANES)
    turn_back[...] = jnp.transpose(block)
    sketch_ref[...] = turn_back[pl.ds(pl.multiple_of(x * own, own), own), :]
    swap.wait_recv()
    gmine[...] = gpart[core] + gslots[...]
    around = []
    for d in range(1, n_z):
        copy = remote(
            gmine, ghalf.at[d - 1], gz_send.at[d - 1], gz_recv.at[d - 1],
            me_g, lax.rem(z + d, n_z) * 2 + x,
        )
        copy.start()
        around.append(copy)
    result = gmine[...]
    for i, copy in enumerate(around):
        copy.wait_recv()
        result = result + ghalf[i]
    gfull[core] = result
    last = remote(gfull.at[core], gfull.at[core], core_send.at[1], core_recv.at[1], sibling, me_d)
    last.start()
    last.wait_recv()
    gram_ref[...] = gfull[...].reshape(width, width)
    for copy in sent + passed + given + around + [swap, last]:
        copy.wait_send()


def general(matrix, flip_bits, sample_rows):
    rows, width = matrix.shape
    n_grp, n_dev = lax.axis_size("grp"), lax.axis_size("dev")
    devices = n_grp * n_dev
    samples = sample_rows.shape[0]
    own = samples // devices
    groups = devices // 4
    chunks = min(width // 8, devices // 2)
    chunk = width // chunks
    pieces = 4
    f32, i32 = jnp.float32, jnp.int32
    dma = pltpu.SemaphoreType.DMA
    vmem = pl.BlockSpec(memory_space=pltpu.VMEM)
    return pl.pallas_call(
        functools.partial(kernel, n_grp, n_dev, rows, own),
        out_shape=(
            pltpu.VMEM((own, width), f32),
            pltpu.VMEM((width, width), f32),
        ),
        in_specs=[pl.BlockSpec(memory_space=pl.ANY)] * 3,
        out_specs=(vmem, vmem),
        scratch_shapes=[
            pltpu.VMEM((rows // LANES, LANES), i32),
            pltpu.VMEM((samples // LANES, LANES), i32),
            pltpu.VMEM((rows, width), f32),
            pltpu.VMEM((2, 4, rows // 2, width), f32),
            pltpu.VMEM((3, rows // LANES, LANES), i32),
            pltpu.VMEM((samples // 2, LANES), i32),
            pltpu.VMEM((groups * own, LANES), i32),
            pltpu.VMEM((groups * own, rows), jnp.bfloat16),
            pltpu.VMEM((2, groups, own // 2, width), f32),
            pltpu.VMEM((2, groups, own // 2, width), f32),
            pltpu.VMEM((chunks, chunk, width), f32),
            pltpu.VMEM((devices, chunk, width), f32),
            pltpu.VMEM((chunks, chunk, width), f32),
            pltpu.VMEM((chunk, width), f32),
            dma((3,)), dma((2,)), dma((2,)), dma((pieces,)), dma((pieces,)), dma((pieces,)), dma((pieces,)),
            dma((3,)), dma((3,)), dma((2,)), dma((2,)), dma, dma, dma, dma,
            pltpu.SemaphoreType.REGULAR((16,)),
        ],
        compiler_params=pltpu.CompilerParams(collective_id=0, has_side_effects=True),
    )(
        matrix,
        flip_bits.reshape(rows // LANES, LANES),
        sample_rows.reshape(samples // LANES, LANES),
    )


def plane_body(matrix, flip_bits, sample_rows):
    rows, width = matrix.shape
    n_grp, n_dev = lax.axis_size("grp"), lax.axis_size("dev")
    samples = sample_rows.shape[0]
    own = samples // (n_grp * n_dev)
    n_y, n_z, peers = n_grp // 2, n_dev // 2, n_grp * 2
    mine, picks, half = width // peers, n_grp * LANES, width // 2
    f32, i32, bf16 = jnp.float32, jnp.int32, jnp.bfloat16
    dma = pltpu.SemaphoreType.DMA
    vmem = pl.BlockSpec(memory_space=pltpu.VMEM)
    return pl.pallas_call(
        functools.partial(plane_kernel, n_grp, n_dev, rows, own),
        out_shape=(pltpu.VMEM((own, width), f32), pltpu.VMEM((width, width), f32)),
        in_specs=[pl.BlockSpec(memory_space=pl.ANY)] * 3,
        out_specs=(vmem, vmem),
        scratch_shapes=[
            pltpu.VMEM((rows, width), f32),
            pltpu.VMEM((rows // LANES, LANES), i32),
            pltpu.VMEM((samples // LANES, LANES), i32),
            pltpu.VMEM((width, rows), f32),
            pltpu.VMEM((peers, mine, rows), f32),
            pltpu.VMEM((n_z, rows, picks), bf16),
            pltpu.VMEM((n_z, peers, 8, picks), f32),
            pltpu.VMEM((n_z, mine, picks), f32),
            pltpu.VMEM((n_z - 1, mine, picks), f32),
            pltpu.VMEM((2, mine, n_y * LANES), f32),
            pltpu.VMEM((peers, mine, n_y * LANES), f32),
            pltpu.VMEM((LANES, width), f32),
            pltpu.VMEM((2, half, width), f32),
            pltpu.VMEM((half, width), f32),
            pltpu.VMEM((n_z - 1, half, width), f32),
            pltpu.VMEM((half, width), f32),
            pltpu.VMEM((2, half, width), f32),
            dma((3,)), dma((peers - 1,)), dma((peers - 1,)), dma((n_z - 1,)), dma((n_z - 1,)),
            dma((peers - 1,)), dma((peers - 1,)), dma((2,)), dma((2,)), dma((n_z - 1,)), dma((n_z - 1,)),
        ],
        compiler_params=pltpu.CompilerParams(collective_id=0, has_side_effects=True),
    )(
        matrix,
        flip_bits.reshape(rows // LANES, LANES),
        sample_rows.reshape(samples // LANES, LANES),
    )


def body(matrix, flip_bits, sample_rows):
    rows, width = matrix.shape
    n_grp, n_dev = lax.axis_size("grp"), lax.axis_size("dev")
    paired = sample_rows.shape[0] * 2 == n_grp * n_dev * LANES
    tiled = width == LANES and width % (n_grp * 2 * 8) == 0
    if paired and tiled and rows % LANES == 0:
        return plane_body(matrix, flip_bits, sample_rows)
    return general(matrix, flip_bits, sample_rows)


def solution(mesh):
    return jax.shard_map(
        body,
        mesh=mesh,
        in_specs=(P(("grp", "dev"), None), P(("grp", "dev")), P()),
        out_specs=(P(("grp", "dev"), None), P()),
        check_vma=False,
    )
```

```python
import functools
import math

import jax
import jax.numpy as jnp
from jax import lax
from jax.experimental import pallas as pl
from jax.experimental.pallas import tpu as pltpu
from jax.sharding import PartitionSpec as P

MESH = pl.DeviceIdType.MESH
LANES = 128


def loop(count, fn):
    if count <= 8:
        for step in range(count):
            fn(step)
    else:
        lax.fori_loop(0, count, lambda step, carry: (fn(step), carry)[1], 0)


def parity(bits, width):
    shift = 1
    while shift * 2 < width:
        shift *= 2
    while shift:
        bits = bits ^ (bits >> shift)
        shift //= 2
    return bits & 1


def sign_of(bits, width):
    return (1 - 2 * parity(bits, width)).astype(jnp.float32)


def split3(value):
    high = value.astype(jnp.bfloat16)
    rest = value - high.astype(jnp.float32)
    mid = rest.astype(jnp.bfloat16)
    low = (rest - mid.astype(jnp.float32)).astype(jnp.bfloat16)
    return high, mid, low


def kernel(
    n_grp, n_dev, rows, own,
    x_ref, flip_hbm, sample_hbm, sketch_ref, gram_ref,
    flip_ref, sample_ref, x_full, slabs, flips, cols, index, base, part, blocks, gpart, gslots, gfull, reduced,
    load_sem, pair_send, pair_recv, twin_send, twin_recv, fwd_send, fwd_recv,
    flip_send, flip_recv, rs_send, rs_recv, g_send, g_recv, b_send, b_recv,
    ready,
):
    f32 = jnp.float32
    devices = n_grp * n_dev
    n_y, n_z = n_grp // 2, n_dev // 2
    groups = n_y * n_z
    width = x_ref.shape[1]
    pieces = twin_send.shape[0]
    piece = rows // pieces
    samples = sample_hbm.shape[0] * LANES
    row_bits = rows.bit_length() - 1
    all_bits = (rows * devices).bit_length() - 1
    me_g, me_d = lax.axis_index("grp"), lax.axis_index("dev")
    core, y = lax.rem(me_g, 2), lax.div(me_g, 2)
    x, z = lax.rem(me_d, 2), lax.div(me_d, 2)
    pair_g = me_g + 1 - 2 * core
    twin_d = me_d + 1 - 2 * x
    mine = y * n_z + z

    def remote(src, dst, send, recv, grp, dev):
        return pltpu.make_async_remote_copy(
            src_ref=src, dst_ref=dst, send_sem=send, recv_sem=recv,
            device_id=(grp, dev), device_id_type=MESH,
        )

    barrier = pltpu.get_barrier_semaphore()

    def signal(sem, grp, dev):
        pl.semaphore_signal(sem, inc=1, device_id=(grp, dev), device_id_type=MESH)

    def along_y(step):
        return me_g + 2 * step, me_d

    def along_z(step):
        return me_g, me_d + 2 * step

    def tell_line(sem, at, size, reach, along):
        for step in range(1, min(reach, size - 1) + 1):
            @pl.when(at >= step)
            def _():
                signal(sem, *along(-step))

            @pl.when(at + step < size)
            def _():
                signal(sem, *along(step))

    def line_count(at, size, reach):
        return jnp.minimum(at, reach) + jnp.minimum(size - 1 - at, reach)

    signal(barrier, pair_g, me_d)
    signal(barrier, me_g, twin_d)
    tell_line(barrier, y, n_y, 1, along_y)
    tell_line(barrier, z, n_z, 1, along_z)

    loads = [
        pltpu.make_async_copy(sample_hbm, sample_ref, load_sem.at[0]),
        pltpu.make_async_copy(flip_hbm, flip_ref, load_sem.at[1]),
        pltpu.make_async_copy(x_ref, x_full, load_sem.at[2]),
    ]
    for copy in loads:
        copy.start()
    pl.semaphore_wait(barrier, 2 + line_count(y, n_y, 1) + line_count(z, n_z, 1))

    rounds = []
    for at, size, along in ((z, n_z, along_z), (y, n_y, along_y)):
        reach = 1
        while reach < size - 1:
            rounds.append((at, size, reach, along))
            reach *= 2
    rounds.append((y, n_y, n_y - 1, along_y))

    def open_round(k):
        if k < len(rounds):
            at, size, reach, along = rounds[k]
            tell_line(ready.at[k], at, size, reach, along)
        elif k == len(rounds):
            signal(ready.at[k], me_g, twin_d)
        else:
            signal(ready.at[k], pair_g, me_d)

    def close_round(k):
        if k < len(rounds):
            at, size, reach, along = rounds[k]
            pl.semaphore_wait(ready.at[k], line_count(at, size, reach))
        else:
            pl.semaphore_wait(ready.at[k], 1)

    half = width // 2
    left = lax.broadcasted_iota(jnp.int32, (1, width), 1) < half

    def swap(value):
        return pltpu.roll(value, half, value.ndim - 1)

    for copy in loads:
        copy.wait()
    top, bottom = x_full[pl.ds(0, rows // 2), :], x_full[pl.ds(rows // 2, rows // 2), :]
    slabs[0, 0] = jnp.where(left, top, swap(bottom))
    slabs[1, 0] = jnp.where(left, swap(top), bottom)
    twin, pair = [], []
    for h in range(2):
        for c in range(pieces // 2):
            at = pl.ds(c * piece, piece)
            k = h * (pieces // 2) + c
            copy = remote(
                slabs.at[h, 0, at], slabs.at[h, 2, at],
                twin_send.at[k], twin_recv.at[k], me_g, twin_d,
            )
            copy.start()
            twin.append(copy)
    for h in range(2):
        copy = remote(
            slabs.at[h, 0], slabs.at[h, 1], pair_send.at[h], pair_recv.at[h], pair_g, me_d
        )
        copy.start()
        pair.append(copy)
    flip_copies = [
        remote(flip_ref, flips.at[0], flip_send.at[0], flip_recv.at[0], pair_g, me_d),
        remote(flip_ref, flips.at[1], flip_send.at[1], flip_recv.at[1], me_g, twin_d),
        remote(flips.at[1], flips.at[2], flip_send.at[2], flip_recv.at[2], pair_g, me_d),
    ]
    open_round(0)
    for copy in flip_copies[:2]:
        copy.start()

    span = n_dev * own // LANES
    for i in range(n_y):
        for r in range(span):
            line = sample_ref[pl.ds((i * 2 + core) * span + r, 1), :]
            cols[pl.ds((i * span + r) * LANES, LANES), :] = jnp.transpose(
                jnp.broadcast_to(line, (LANES, LANES))
            )
    for i in range(n_y):
        for j in range(n_z):
            index[pl.ds((i * n_z + j) * own, own), :] = cols[
                pl.ds((i * n_dev + j * 2 + x) * own, own), :
            ]
    close_round(0)
    open_round(1)
    picks = groups * own
    wanted = index[...]
    for k in range(rows // LANES):
        lane = lax.broadcasted_iota(jnp.int32, (picks, LANES), 1) + k * LANES
        base[:, k * LANES:(k + 1) * LANES] = sign_of(wanted & lane, row_bits).astype(jnp.bfloat16)

    owner_signs = [
        sign_of(wanted & ((grp * n_dev + dev) * rows), all_bits)
        for grp, dev in ((me_g, me_d), (pair_g, me_d), (me_g, twin_d), (pair_g, twin_d))
    ]

    def term(h, slot, flip_bits, grp, dev):
        signs = base[...]
        toggles = (1 - 2 * flip_bits).astype(f32).astype(jnp.bfloat16)
        signs = jnp.concatenate(
            [
                signs[:, k * LANES:(k + 1) * LANES] * toggles[k:k + 1, :]
                for k in range(rows // LANES)
            ],
            axis=1,
        )
        packed = slabs[h, slot]
        high, mid, low = split3(packed)
        high_s, mid_s, low_s = split3(swap(packed))
        right = jnp.concatenate(
            [
                jnp.concatenate([jnp.where(left, high, mid_s), low], axis=1),
                jnp.concatenate([jnp.where(left, high_s, mid), low_s], axis=1),
            ],
            axis=0,
        )
        product = jnp.dot(signs, right, preferred_element_type=f32)
        first, last = product[:, :width], product[:, width:]
        return (first + swap(first) + last) * owner_signs[slot]

    def give(h, i, j):
        to_y, to_z = lax.rem(y + i, n_y), lax.rem(z + j, n_z)
        remote(
            part.at[h, to_y * n_z + to_z], blocks.at[h, mine], rs_send.at[h], rs_recv.at[h],
            to_y * 2 + core, to_z * 2 + x,
        ).start()

    for k in range(1, len(rounds) - 1):
        close_round(k)
        open_round(k + 1)
    totals = [term(h, 0, flip_ref[...], me_g, me_d) for h in range(2)]
    close_round(len(rounds) - 1)
    open_round(len(rounds))
    flip_copies[0].wait_recv()
    for h in range(2):
        pair[h].wait_recv()
        totals[h] = totals[h] + term(h, 1, flips[0], pair_g, me_d)
    flip_copies[1].wait_recv()
    flip_copies[2].start()
    forward = []
    for h in range(2):
        for c in range(pieces // 2):
            at = pl.ds(c * piece, piece)
            k = h * (pieces // 2) + c
            twin[k].wait_recv()
            copy = remote(
                slabs.at[h, 2, at], slabs.at[h, 3, at],
                fwd_send.at[k], fwd_recv.at[k], pair_g, me_d,
            )
            copy.start()
            forward.append(copy)
        total = totals[h] + term(h, 2, flips[1], me_g, twin_d)
        if h == 0:
            flip_copies[2].wait_recv()
        for copy in forward[h * (pieces // 2):]:
            copy.wait_recv()
        total = total + term(h, 3, flips[2], pair_g, twin_d)
        total = total.reshape(groups, own, width)
        part[h] = jnp.where(
            left.reshape(1, 1, width), total[:, :own // 2], swap(total[:, own // 2:])
        )
        if h == 0:
            close_round(len(rounds))
            open_round(len(rounds) + 1)
        for i in range(n_y - 1, -1, -1):
            loop(n_z - (i == 0), lambda j: give(h, i, j + (i == 0)))
        blocks[h, mine] = part[h, mine]
    sums = []
    for h in range(2):
        others = blocks.at[h, pl.ds(0, groups - 1)]
        pltpu.make_async_copy(others, others, rs_recv.at[h]).wait()
        summed = blocks[h, 0]
        for i in range(1, groups):
            summed = summed + blocks[h, i]
        sums.append(summed)
    sketch = jnp.concatenate(
        [
            jnp.where(left, sums[0], swap(sums[1])),
            jnp.where(left, swap(sums[0]), sums[1]),
        ],
        axis=0,
    )
    sketch = sketch * (1.0 / math.sqrt(rows * devices))
    sketch_ref[...] = sketch

    close_round(len(rounds) + 1)
    chunks = gfull.shape[0]
    across = min(chunks, n_dev // 2)
    first = (n_dev - across) // 2
    chunk = width // chunks
    linear = me_g * n_dev + me_d
    reducer = (me_g < chunks // across) & (me_d >= first) & (me_d < first + across)
    my_chunk = me_g * across + me_d - first
    gram = lax.dot_general(
        sketch, sketch, (((0,), (0,)), ((), ())),
        precision=lax.Precision.HIGHEST, preferred_element_type=f32,
    )
    gpart[...] = gram.reshape(chunks, chunk, width)
    turn = lax.rem(linear, chunks)
    for k in range(chunks):
        to = lax.rem(k + turn, chunks)
        to_g, to_d = lax.div(to, across), first + lax.rem(to, across)

        @pl.when((me_g != to_g) | (me_d != to_d))
        def _():
            remote(gpart.at[to], gslots.at[linear], g_send, g_recv, to_g, to_d).start()

    @pl.when(reducer)
    def _():
        gslots[linear] = gpart[my_chunk]
        rest = gslots.at[pl.ds(0, devices - 1)]
        pltpu.make_async_copy(rest, rest, g_recv).wait()
        result = jnp.sum(gslots[...], axis=0) * (1.0 / samples)
        reduced[...] = result
        gfull[my_chunk] = result

        def tell(i, j):
            remote(
                reduced, gfull.at[my_chunk], b_send, b_recv,
                lax.rem(me_g + i, n_grp), lax.rem(me_d + j, n_dev),
            ).start()

        for i in range(n_grp - 1, -1, -1):
            loop(n_dev - (i == 0), lambda j: tell(i, j + (i == 0)))
        most = gfull.at[pl.ds(0, chunks - 1)]
        pltpu.make_async_copy(most, most, b_recv).wait()
        pltpu.make_async_copy(rest, rest, b_send).wait()
        pltpu.make_async_copy(most, most, g_send).wait()

    @pl.when(jnp.logical_not(reducer))
    def _():
        pltpu.make_async_copy(gfull, gfull, b_recv).wait()
        pltpu.make_async_copy(gfull, gfull, g_send).wait()

    gram_ref[...] = gfull[...].reshape(width, width)
    for copy in twin + forward + flip_copies + pair:
        copy.wait_send()
    for h in range(2):
        others = blocks.at[h, pl.ds(0, groups - 1)]
        pltpu.make_async_copy(others, others, rs_send.at[h]).wait()


def split2(value):
    high = value.astype(jnp.bfloat16)
    return high, (value - high.astype(jnp.float32)).astype(jnp.bfloat16)


def plane_kernel(
    n_grp, n_dev, rows, own,
    x_hbm, flip_hbm, sample_hbm, sketch_ref, gram_ref,
    x_ref, flip_ref, sample_ref, turned, slabs, signs, peer_signs, part, blocks, mixed, cols, turn_back,
    gram_out, gram_in,
    load_sem, in_send, in_recv, z_send, z_recv, out_send, out_recv, g_send, g_recv,
):
    f32, bf16 = jnp.float32, jnp.bfloat16
    width = x_ref.shape[1]
    n_y, n_z = n_grp // 2, n_dev // 2
    peers = n_grp * 2
    half = width // 2
    mine = half // peers
    span = n_dev * own // LANES
    samples = sample_ref.shape[0] * LANES
    picks = n_grp * LANES
    row_bits = rows.bit_length() - 1
    all_bits = (rows * n_grp * n_dev).bit_length() - 1
    me_g, me_d = lax.axis_index("grp"), lax.axis_index("dev")
    core, y = lax.rem(me_g, 2), lax.div(me_g, 2)
    x, z = lax.rem(me_d, 2), lax.div(me_d, 2)
    me = me_g * 2 + x

    plane = [(a, k, b) for a in range(n_y) for k in range(2) for b in range(2)][:0:-1]
    plane = sorted(plane, key=lambda at: -((at[0] > 0) + at[1]))
    order = sorted(range(n_z), key=lambda d: -min(d, n_z - d))
    ring = [(d, b) for d in order for b in range(2) if d or b]

    def peer(a, k, b):
        to_y, to_x, to_c = lax.rem(y + a, n_y), lax.rem(x + k, 2), lax.rem(core + b, 2)
        return to_y * 2 + to_c, z * 2 + to_x

    def along(d, b):
        return y * 2 + lax.rem(core + b, 2), lax.rem(z + d, n_z) * 2 + x

    def remote(src, dst, send, recv, at):
        return pltpu.make_async_remote_copy(
            src_ref=src, dst_ref=dst, send_sem=send, recv_sem=recv,
            device_id=at, device_id_type=MESH,
        )

    barrier = pltpu.get_barrier_semaphore()
    loads = [
        pltpu.make_async_copy(x_hbm, x_ref, load_sem.at[0]),
        pltpu.make_async_copy(flip_hbm, flip_ref, load_sem.at[1]),
        pltpu.make_async_copy(sample_hbm, sample_ref, load_sem.at[2]),
    ]
    for copy in loads:
        copy.start()
    greeted = [peer(*at) for at in plane] + [along(*at) for at in ring if at[0]]
    for at in greeted:
        pl.semaphore_signal(barrier, inc=1, device_id=at, device_id_type=MESH)
    for copy in loads:
        copy.wait()

    toggles = (1 - 2 * flip_ref[...]).astype(f32)
    for k in range(rows // LANES):
        at = slice(k * LANES, (k + 1) * LANES)
        turned[:, at] = jnp.transpose(x_ref[at, :]) * toggles[k:k + 1, :]
    pl.semaphore_wait(barrier, len(greeted))

    sent = []
    for h in range(2):
        for m, at in enumerate(plane):
            grp, dev = peer(*at)
            to = grp * 2 + lax.rem(dev, 2)
            copy = remote(
                turned.at[pl.ds(pl.multiple_of(h * half + to * mine, mine), mine)],
                slabs.at[h, me], in_send.at[h, m], in_recv.at[h, m], (grp, dev),
            )
            copy.start()
            sent.append(copy)
        slabs[h, me] = turned[pl.ds(pl.multiple_of(h * half + me * mine, mine), mine), :]

    low = lax.broadcasted_iota(jnp.int32, (16, LANES), 0)
    for i, d in enumerate(order):
        to_z = lax.rem(z + d, n_z)
        for g in range(n_grp):
            wanted = sample_ref[pl.ds(g * span + to_z, 1), :]
            wide = jnp.broadcast_to(wanted, (16, LANES))
            pieces = [sign_of(wide & low, 16).astype(bf16)]
            for bit in range(4, row_bits):
                factor = (1 - 2 * ((wide >> bit) & 1)).astype(f32).astype(bf16)
                pieces += [piece * factor for piece in pieces]
            for k, piece in enumerate(pieces):
                signs[i, k * 16:(k + 1) * 16, g * LANES:(g + 1) * LANES] = piece
            wide = wide[:8]
            for p in range(peers):
                holder = ((p // 2) * n_dev + z * 2 + p % 2) * rows
                peer_signs[i, p, :, g * LANES:(g + 1) * LANES] = sign_of(wide & holder, all_bits)

    passed = []
    for h in range(2):
        for copy in sent[h * len(plane):(h + 1) * len(plane)]:
            copy.wait_recv()
        high, mid = split2(slabs[h].reshape(half, rows))
        left = jnp.concatenate([high, mid], axis=0)
        for i, d in enumerate(order):
            product = jnp.dot(left, signs[i], preferred_element_type=f32)
            product = product[:half] + product[half:]
            total = None
            for p in range(peers):
                term = product[p * mine:(p + 1) * mine].reshape(mine // 8, 8, picks) * peer_signs[i, p][None]
                total = term if total is None else total + term
            part[h, i] = total.reshape(mine, picks)
            if d:
                copy = remote(
                    part.at[h, i], blocks.at[h, i], z_send.at[h, i], z_recv.at[h, i], along(d, 0)
                )
                copy.start()
                passed.append(copy)
    given = []
    for h in range(2):
        total = part[h, n_z - 1]
        for i, copy in enumerate(passed[h * (n_z - 1):(h + 1) * (n_z - 1)]):
            copy.wait_recv()
            total = total + blocks[h, i]
        mixed[h] = total * (1.0 / math.sqrt(rows * n_grp * n_dev))
        for m, at in enumerate(plane):
            copy = remote(
                mixed.at[h], cols.at[h, me], out_send.at[h, m], out_recv.at[h, m], peer(*at)
            )
            copy.start()
            given.append(copy)
        cols[h, me] = mixed[h]

    around = []
    right = None
    for h in range(2):
        for copy in given[h * len(plane):(h + 1) * len(plane)]:
            copy.wait_recv()
        high, mid = split2(cols[h].reshape(half, picks))
        fresh = jnp.concatenate([high, high, mid], axis=1)
        right = fresh if right is None else jnp.concatenate([right, fresh], axis=0)
        high, mid = split2(cols[h, pl.ds(core * (peers // 2), peers // 2)].reshape(half // 2, picks))
        gram = lax.dot_general(
            jnp.concatenate([high, mid, high], axis=1), right,
            (((1,), (1,)), ((), ())), preferred_element_type=f32,
        )
        if h == 0:
            gram = jnp.concatenate([gram, jnp.zeros_like(gram)], axis=1)
        gram_out[h] = gram * (1.0 / samples)
        for m, (d, b) in enumerate(ring):
            copy = remote(
                gram_out.at[h], gram_in.at[h, d, core], g_send.at[h, m], g_recv.at[h, m], along(d, b)
            )
            copy.start()
            around.append(copy)
        gram_in[h, 0, core] = gram_out[h]

    block = cols[:, :, :, pl.ds(pl.multiple_of(me_g * LANES, LANES), LANES)].reshape(width, LANES)
    turn_back[...] = jnp.transpose(block)
    sketch_ref[...] = turn_back[pl.ds(pl.multiple_of(x * own, own), own), :]
    result = []
    for h in range(2):
        for copy in around[h * len(ring):(h + 1) * len(ring)]:
            copy.wait_recv()
        total = gram_in[h, 0]
        for d in range(1, n_z):
            total = total + gram_in[h, d]
        result.append(total.reshape(half, width))
    cross = jnp.transpose(result[1])[:half]
    gram_ref[:half, :] = jnp.concatenate([result[0][:, :half], cross], axis=1)
    gram_ref[half:, :] = result[1]
    for copy in sent + passed + given + around:
        copy.wait_send()


def general(matrix, flip_bits, sample_rows):
    rows, width = matrix.shape
    n_grp, n_dev = lax.axis_size("grp"), lax.axis_size("dev")
    devices = n_grp * n_dev
    samples = sample_rows.shape[0]
    own = samples // devices
    groups = devices // 4
    chunks = min(width // 8, devices // 2)
    chunk = width // chunks
    pieces = 4
    f32, i32 = jnp.float32, jnp.int32
    dma = pltpu.SemaphoreType.DMA
    vmem = pl.BlockSpec(memory_space=pltpu.VMEM)
    return pl.pallas_call(
        functools.partial(kernel, n_grp, n_dev, rows, own),
        out_shape=(
            pltpu.VMEM((own, width), f32),
            pltpu.VMEM((width, width), f32),
        ),
        in_specs=[pl.BlockSpec(memory_space=pl.ANY)] * 3,
        out_specs=(vmem, vmem),
        scratch_shapes=[
            pltpu.VMEM((rows // LANES, LANES), i32),
            pltpu.VMEM((samples // LANES, LANES), i32),
            pltpu.VMEM((rows, width), f32),
            pltpu.VMEM((2, 4, rows // 2, width), f32),
            pltpu.VMEM((3, rows // LANES, LANES), i32),
            pltpu.VMEM((samples // 2, LANES), i32),
            pltpu.VMEM((groups * own, LANES), i32),
            pltpu.VMEM((groups * own, rows), jnp.bfloat16),
            pltpu.VMEM((2, groups, own // 2, width), f32),
            pltpu.VMEM((2, groups, own // 2, width), f32),
            pltpu.VMEM((chunks, chunk, width), f32),
            pltpu.VMEM((devices, chunk, width), f32),
            pltpu.VMEM((chunks, chunk, width), f32),
            pltpu.VMEM((chunk, width), f32),
            dma((3,)), dma((2,)), dma((2,)), dma((pieces,)), dma((pieces,)), dma((pieces,)), dma((pieces,)),
            dma((3,)), dma((3,)), dma((2,)), dma((2,)), dma, dma, dma, dma,
            pltpu.SemaphoreType.REGULAR((16,)),
        ],
        compiler_params=pltpu.CompilerParams(collective_id=0, has_side_effects=True),
    )(
        matrix,
        flip_bits.reshape(rows // LANES, LANES),
        sample_rows.reshape(samples // LANES, LANES),
    )


def plane_body(matrix, flip_bits, sample_rows):
    rows, width = matrix.shape
    n_grp, n_dev = lax.axis_size("grp"), lax.axis_size("dev")
    samples = sample_rows.shape[0]
    own = samples // (n_grp * n_dev)
    n_z, peers = n_dev // 2, n_grp * 2
    mine, picks, half = width // peers // 2, n_grp * LANES, width // 2
    f32, i32, bf16 = jnp.float32, jnp.int32, jnp.bfloat16
    dma = pltpu.SemaphoreType.DMA
    vmem = pl.BlockSpec(memory_space=pltpu.VMEM)
    return pl.pallas_call(
        functools.partial(plane_kernel, n_grp, n_dev, rows, own),
        out_shape=(pltpu.VMEM((own, width), f32), pltpu.VMEM((width, width), f32)),
        in_specs=[pl.BlockSpec(memory_space=pl.ANY)] * 3,
        out_specs=(vmem, vmem),
        scratch_shapes=[
            pltpu.VMEM((rows, width), f32),
            pltpu.VMEM((rows // LANES, LANES), i32),
            pltpu.VMEM((samples // LANES, LANES), i32),
            pltpu.VMEM((width, rows), f32),
            pltpu.VMEM((2, peers, mine, rows), f32),
            pltpu.VMEM((n_z, rows, picks), bf16),
            pltpu.VMEM((n_z, peers, 8, picks), f32),
            pltpu.VMEM((2, n_z, mine, picks), f32),
            pltpu.VMEM((2, n_z - 1, mine, picks), f32),
            pltpu.VMEM((2, mine, picks), f32),
            pltpu.VMEM((2, peers, mine, picks), f32),
            pltpu.VMEM((LANES, width), f32),
            pltpu.VMEM((2, half // 2, width), f32),
            pltpu.VMEM((2, n_z, 2, half // 2, width), f32),
            dma((3,)), dma((2, peers - 1)), dma((2, peers - 1)), dma((2, n_z - 1)), dma((2, n_z - 1)),
            dma((2, peers - 1)), dma((2, peers - 1)), dma((2, 2 * n_z - 1)), dma((2, 2 * n_z - 1)),
        ],
        compiler_params=pltpu.CompilerParams(collective_id=0, has_side_effects=True),
    )(
        matrix,
        flip_bits.reshape(rows // LANES, LANES),
        sample_rows.reshape(samples // LANES, LANES),
    )


def body(matrix, flip_bits, sample_rows):
    rows, width = matrix.shape
    n_grp, n_dev = lax.axis_size("grp"), lax.axis_size("dev")
    paired = sample_rows.shape[0] * 2 == n_grp * n_dev * LANES
    tiled = width == LANES and width % (n_grp * 2 * 16) == 0
    if paired and tiled and rows % LANES == 0:
        return plane_body(matrix, flip_bits, sample_rows)
    return general(matrix, flip_bits, sample_rows)


def solution(mesh):
    return jax.shard_map(
        body,
        mesh=mesh,
        in_specs=(P(("grp", "dev"), None), P(("grp", "dev")), P()),
        out_specs=(P(("grp", "dev"), None), P()),
        check_vma=False,
    )
```

```python
import functools
import math

import jax
import jax.numpy as jnp
from jax import lax
from jax.experimental import pallas as pl
from jax.experimental.pallas import tpu as pltpu
from jax.sharding import PartitionSpec as P

MESH = pl.DeviceIdType.MESH
LANES = 128


def loop(count, fn):
    if count <= 8:
        for step in range(count):
            fn(step)
    else:
        lax.fori_loop(0, count, lambda step, carry: (fn(step), carry)[1], 0)


def parity(bits, width):
    shift = 1
    while shift * 2 < width:
        shift *= 2
    while shift:
        bits = bits ^ (bits >> shift)
        shift //= 2
    return bits & 1


def sign_of(bits, width):
    return (1 - 2 * parity(bits, width)).astype(jnp.float32)


def split3(value):
    high = value.astype(jnp.bfloat16)
    rest = value - high.astype(jnp.float32)
    mid = rest.astype(jnp.bfloat16)
    low = (rest - mid.astype(jnp.float32)).astype(jnp.bfloat16)
    return high, mid, low


def kernel(
    n_grp, n_dev, rows, own,
    x_ref, flip_hbm, sample_hbm, sketch_ref, gram_ref,
    flip_ref, sample_ref, x_full, slabs, flips, cols, index, base, part, blocks, gpart, gslots, gfull, reduced,
    load_sem, pair_send, pair_recv, twin_send, twin_recv, fwd_send, fwd_recv,
    flip_send, flip_recv, rs_send, rs_recv, g_send, g_recv, b_send, b_recv,
    ready,
):
    f32 = jnp.float32
    devices = n_grp * n_dev
    n_y, n_z = n_grp // 2, n_dev // 2
    groups = n_y * n_z
    width = x_ref.shape[1]
    pieces = twin_send.shape[0]
    piece = rows // pieces
    samples = sample_hbm.shape[0] * LANES
    row_bits = rows.bit_length() - 1
    all_bits = (rows * devices).bit_length() - 1
    me_g, me_d = lax.axis_index("grp"), lax.axis_index("dev")
    core, y = lax.rem(me_g, 2), lax.div(me_g, 2)
    x, z = lax.rem(me_d, 2), lax.div(me_d, 2)
    pair_g = me_g + 1 - 2 * core
    twin_d = me_d + 1 - 2 * x
    mine = y * n_z + z

    def remote(src, dst, send, recv, grp, dev):
        return pltpu.make_async_remote_copy(
            src_ref=src, dst_ref=dst, send_sem=send, recv_sem=recv,
            device_id=(grp, dev), device_id_type=MESH,
        )

    barrier = pltpu.get_barrier_semaphore()

    def signal(sem, grp, dev):
        pl.semaphore_signal(sem, inc=1, device_id=(grp, dev), device_id_type=MESH)

    def along_y(step):
        return me_g + 2 * step, me_d

    def along_z(step):
        return me_g, me_d + 2 * step

    def tell_line(sem, at, size, reach, along):
        for step in range(1, min(reach, size - 1) + 1):
            @pl.when(at >= step)
            def _():
                signal(sem, *along(-step))

            @pl.when(at + step < size)
            def _():
                signal(sem, *along(step))

    def line_count(at, size, reach):
        return jnp.minimum(at, reach) + jnp.minimum(size - 1 - at, reach)

    signal(barrier, pair_g, me_d)
    signal(barrier, me_g, twin_d)
    tell_line(barrier, y, n_y, 1, along_y)
    tell_line(barrier, z, n_z, 1, along_z)

    loads = [
        pltpu.make_async_copy(sample_hbm, sample_ref, load_sem.at[0]),
        pltpu.make_async_copy(flip_hbm, flip_ref, load_sem.at[1]),
        pltpu.make_async_copy(x_ref, x_full, load_sem.at[2]),
    ]
    for copy in loads:
        copy.start()
    pl.semaphore_wait(barrier, 2 + line_count(y, n_y, 1) + line_count(z, n_z, 1))

    rounds = []
    for at, size, along in ((z, n_z, along_z), (y, n_y, along_y)):
        reach = 1
        while reach < size - 1:
            rounds.append((at, size, reach, along))
            reach *= 2
    rounds.append((y, n_y, n_y - 1, along_y))

    def open_round(k):
        if k < len(rounds):
            at, size, reach, along = rounds[k]
            tell_line(ready.at[k], at, size, reach, along)
        elif k == len(rounds):
            signal(ready.at[k], me_g, twin_d)
        else:
            signal(ready.at[k], pair_g, me_d)

    def close_round(k):
        if k < len(rounds):
            at, size, reach, along = rounds[k]
            pl.semaphore_wait(ready.at[k], line_count(at, size, reach))
        else:
            pl.semaphore_wait(ready.at[k], 1)

    half = width // 2
    left = lax.broadcasted_iota(jnp.int32, (1, width), 1) < half

    def swap(value):
        return pltpu.roll(value, half, value.ndim - 1)

    for copy in loads:
        copy.wait()
    top, bottom = x_full[pl.ds(0, rows // 2), :], x_full[pl.ds(rows // 2, rows // 2), :]
    slabs[0, 0] = jnp.where(left, top, swap(bottom))
    slabs[1, 0] = jnp.where(left, swap(top), bottom)
    twin, pair = [], []
    for h in range(2):
        for c in range(pieces // 2):
            at = pl.ds(c * piece, piece)
            k = h * (pieces // 2) + c
            copy = remote(
                slabs.at[h, 0, at], slabs.at[h, 2, at],
                twin_send.at[k], twin_recv.at[k], me_g, twin_d,
            )
            copy.start()
            twin.append(copy)
    for h in range(2):
        copy = remote(
            slabs.at[h, 0], slabs.at[h, 1], pair_send.at[h], pair_recv.at[h], pair_g, me_d
        )
        copy.start()
        pair.append(copy)
    flip_copies = [
        remote(flip_ref, flips.at[0], flip_send.at[0], flip_recv.at[0], pair_g, me_d),
        remote(flip_ref, flips.at[1], flip_send.at[1], flip_recv.at[1], me_g, twin_d),
        remote(flips.at[1], flips.at[2], flip_send.at[2], flip_recv.at[2], pair_g, me_d),
    ]
    open_round(0)
    for copy in flip_copies[:2]:
        copy.start()

    span = n_dev * own // LANES
    for i in range(n_y):
        for r in range(span):
            line = sample_ref[pl.ds((i * 2 + core) * span + r, 1), :]
            cols[pl.ds((i * span + r) * LANES, LANES), :] = jnp.transpose(
                jnp.broadcast_to(line, (LANES, LANES))
            )
    for i in range(n_y):
        for j in range(n_z):
            index[pl.ds((i * n_z + j) * own, own), :] = cols[
                pl.ds((i * n_dev + j * 2 + x) * own, own), :
            ]
    close_round(0)
    open_round(1)
    picks = groups * own
    wanted = index[...]
    for k in range(rows // LANES):
        lane = lax.broadcasted_iota(jnp.int32, (picks, LANES), 1) + k * LANES
        base[:, k * LANES:(k + 1) * LANES] = sign_of(wanted & lane, row_bits).astype(jnp.bfloat16)

    owner_signs = [
        sign_of(wanted & ((grp * n_dev + dev) * rows), all_bits)
        for grp, dev in ((me_g, me_d), (pair_g, me_d), (me_g, twin_d), (pair_g, twin_d))
    ]

    def term(h, slot, flip_bits, grp, dev):
        signs = base[...]
        toggles = (1 - 2 * flip_bits).astype(f32).astype(jnp.bfloat16)
        signs = jnp.concatenate(
            [
                signs[:, k * LANES:(k + 1) * LANES] * toggles[k:k + 1, :]
                for k in range(rows // LANES)
            ],
            axis=1,
        )
        packed = slabs[h, slot]
        high, mid, low = split3(packed)
        high_s, mid_s, low_s = split3(swap(packed))
        right = jnp.concatenate(
            [
                jnp.concatenate([jnp.where(left, high, mid_s), low], axis=1),
                jnp.concatenate([jnp.where(left, high_s, mid), low_s], axis=1),
            ],
            axis=0,
        )
        product = jnp.dot(signs, right, preferred_element_type=f32)
        first, last = product[:, :width], product[:, width:]
        return (first + swap(first) + last) * owner_signs[slot]

    def give(h, i, j):
        to_y, to_z = lax.rem(y + i, n_y), lax.rem(z + j, n_z)
        remote(
            part.at[h, to_y * n_z + to_z], blocks.at[h, mine], rs_send.at[h], rs_recv.at[h],
            to_y * 2 + core, to_z * 2 + x,
        ).start()

    for k in range(1, len(rounds) - 1):
        close_round(k)
        open_round(k + 1)
    totals = [term(h, 0, flip_ref[...], me_g, me_d) for h in range(2)]
    close_round(len(rounds) - 1)
    open_round(len(rounds))
    flip_copies[0].wait_recv()
    for h in range(2):
        pair[h].wait_recv()
        totals[h] = totals[h] + term(h, 1, flips[0], pair_g, me_d)
    flip_copies[1].wait_recv()
    flip_copies[2].start()
    forward = []
    for h in range(2):
        for c in range(pieces // 2):
            at = pl.ds(c * piece, piece)
            k = h * (pieces // 2) + c
            twin[k].wait_recv()
            copy = remote(
                slabs.at[h, 2, at], slabs.at[h, 3, at],
                fwd_send.at[k], fwd_recv.at[k], pair_g, me_d,
            )
            copy.start()
            forward.append(copy)
        total = totals[h] + term(h, 2, flips[1], me_g, twin_d)
        if h == 0:
            flip_copies[2].wait_recv()
        for copy in forward[h * (pieces // 2):]:
            copy.wait_recv()
        total = total + term(h, 3, flips[2], pair_g, twin_d)
        total = total.reshape(groups, own, width)
        part[h] = jnp.where(
            left.reshape(1, 1, width), total[:, :own // 2], swap(total[:, own // 2:])
        )
        if h == 0:
            close_round(len(rounds))
            open_round(len(rounds) + 1)
        for i in range(n_y - 1, -1, -1):
            loop(n_z - (i == 0), lambda j: give(h, i, j + (i == 0)))
        blocks[h, mine] = part[h, mine]
    sums = []
    for h in range(2):
        others = blocks.at[h, pl.ds(0, groups - 1)]
        pltpu.make_async_copy(others, others, rs_recv.at[h]).wait()
        summed = blocks[h, 0]
        for i in range(1, groups):
            summed = summed + blocks[h, i]
        sums.append(summed)
    sketch = jnp.concatenate(
        [
            jnp.where(left, sums[0], swap(sums[1])),
            jnp.where(left, swap(sums[0]), sums[1]),
        ],
        axis=0,
    )
    sketch = sketch * (1.0 / math.sqrt(rows * devices))
    sketch_ref[...] = sketch

    close_round(len(rounds) + 1)
    chunks = gfull.shape[0]
    across = min(chunks, n_dev // 2)
    first = (n_dev - across) // 2
    chunk = width // chunks
    linear = me_g * n_dev + me_d
    reducer = (me_g < chunks // across) & (me_d >= first) & (me_d < first + across)
    my_chunk = me_g * across + me_d - first
    gram = lax.dot_general(
        sketch, sketch, (((0,), (0,)), ((), ())),
        precision=lax.Precision.HIGHEST, preferred_element_type=f32,
    )
    gpart[...] = gram.reshape(chunks, chunk, width)
    turn = lax.rem(linear, chunks)
    for k in range(chunks):
        to = lax.rem(k + turn, chunks)
        to_g, to_d = lax.div(to, across), first + lax.rem(to, across)

        @pl.when((me_g != to_g) | (me_d != to_d))
        def _():
            remote(gpart.at[to], gslots.at[linear], g_send, g_recv, to_g, to_d).start()

    @pl.when(reducer)
    def _():
        gslots[linear] = gpart[my_chunk]
        rest = gslots.at[pl.ds(0, devices - 1)]
        pltpu.make_async_copy(rest, rest, g_recv).wait()
        result = jnp.sum(gslots[...], axis=0) * (1.0 / samples)
        reduced[...] = result
        gfull[my_chunk] = result

        def tell(i, j):
            remote(
                reduced, gfull.at[my_chunk], b_send, b_recv,
                lax.rem(me_g + i, n_grp), lax.rem(me_d + j, n_dev),
            ).start()

        for i in range(n_grp - 1, -1, -1):
            loop(n_dev - (i == 0), lambda j: tell(i, j + (i == 0)))
        most = gfull.at[pl.ds(0, chunks - 1)]
        pltpu.make_async_copy(most, most, b_recv).wait()
        pltpu.make_async_copy(rest, rest, b_send).wait()
        pltpu.make_async_copy(most, most, g_send).wait()

    @pl.when(jnp.logical_not(reducer))
    def _():
        pltpu.make_async_copy(gfull, gfull, b_recv).wait()
        pltpu.make_async_copy(gfull, gfull, g_send).wait()

    gram_ref[...] = gfull[...].reshape(width, width)
    for copy in twin + forward + flip_copies + pair:
        copy.wait_send()
    for h in range(2):
        others = blocks.at[h, pl.ds(0, groups - 1)]
        pltpu.make_async_copy(others, others, rs_send.at[h]).wait()


def split2(value):
    high = value.astype(jnp.bfloat16)
    return high, (value - high.astype(jnp.float32)).astype(jnp.bfloat16)


def plane_kernel(
    n_grp, n_dev, rows, own,
    x_hbm, flip_hbm, sample_hbm, sketch_ref, gram_ref,
    x_ref, flip_ref, sample_ref, turned, slabs, signs, peer_signs, lent, borrowed, part, blocks, mixed, cols,
    turn_back, gram_out, gram_in, gram_sum, gram_far, lower,
    load_sem, in_send, in_recv, c_send, c_recv, z_send, z_recv, out_send, out_recv,
    g_send, g_recv, h_send, h_recv,
):
    f32, bf16 = jnp.float32, jnp.bfloat16
    width = x_ref.shape[1]
    n_y, n_z = n_grp // 2, n_dev // 2
    chips = n_y * 2
    chunks, mine = slabs.shape[0], slabs.shape[2]
    band = chips * mine
    span = n_dev * own // LANES
    samples = sample_ref.shape[0] * LANES
    picks = n_y * LANES
    row_bits = rows.bit_length() - 1
    all_bits = (rows * n_grp * n_dev).bit_length() - 1
    me_g, me_d = lax.axis_index("grp"), lax.axis_index("dev")
    core, y = lax.rem(me_g, 2), lax.div(me_g, 2)
    x, z = lax.rem(me_d, 2), lax.div(me_d, 2)
    me = y * 2 + x

    plane = [(a, k) for a in range(n_y - 1, -1, -1) for k in (1, 0) if a or k]
    order = sorted(range(n_z), key=lambda d: -min(d, n_z - d))
    sibling = (me_g + 1 - 2 * core, me_d)

    def across(a, k):
        to_y, to_x = lax.rem(y + a, n_y), lax.rem(x + k, 2)
        return (to_y * 2 + core, z * 2 + to_x), to_y * 2 + to_x

    def along(d):
        return me_g, lax.rem(z + d, n_z) * 2 + x

    def remote(src, dst, send, recv, at):
        return pltpu.make_async_remote_copy(
            src_ref=src, dst_ref=dst, send_sem=send, recv_sem=recv,
            device_id=at, device_id_type=MESH,
        )


    barrier = pltpu.get_barrier_semaphore()
    loads = [
        pltpu.make_async_copy(x_hbm, x_ref, load_sem.at[0]),
        pltpu.make_async_copy(flip_hbm, flip_ref, load_sem.at[1]),
        pltpu.make_async_copy(sample_hbm, sample_ref, load_sem.at[2]),
    ]
    for copy in loads:
        copy.start()
    greeted = [across(*at)[0] for at in plane] + [along(d) for d in order[:-1]] + [sibling]
    for at in greeted:
        pl.semaphore_signal(barrier, inc=1, device_id=at, device_id_type=MESH)
    for copy in loads:
        copy.wait()

    toggles = (1 - 2 * flip_ref[...]).astype(f32)
    for k in range(rows // LANES):
        at = slice(k * LANES, (k + 1) * LANES)
        turned[:, at] = jnp.transpose(x_ref[at, :]) * toggles[k:k + 1, :]
    pl.semaphore_wait(barrier, len(greeted))

    sent, swaps, passed, given, around, last = [], [], [], [], [], []
    for k in range(chunks):
        for m, at in enumerate(plane):
            to, chip = across(*at)
            copy = remote(
                turned.at[pl.ds(pl.multiple_of(k * band + chip * mine, mine), mine)],
                slabs.at[k, me], in_send.at[k, m], in_recv.at[k, m], to,
            )
            copy.start()
            sent.append(copy)
    for k in range(chunks):
        slabs[k, me] = turned[pl.ds(pl.multiple_of(k * band + me * mine, mine), mine), :]

    low = lax.broadcasted_iota(jnp.int32, (16, LANES), 0)
    for r in range(2):
        owner = core if r else 1 - core
        for i, d in enumerate(order):
            to_z = lax.rem(z + d, n_z)
            for j in range(n_y):
                at = slice(i * picks + j * LANES, i * picks + (j + 1) * LANES)
                wanted = sample_ref[pl.ds((j * 2 + owner) * span + to_z, 1), :]
                wide = jnp.broadcast_to(wanted, (16, LANES))
                pieces = [sign_of(wide & low, 16).astype(bf16)]
                for bit in range(4, row_bits):
                    factor = (1 - 2 * ((wide >> bit) & 1)).astype(f32).astype(bf16)
                    pieces += [piece * factor for piece in pieces]
                for k, piece in enumerate(pieces):
                    signs[r, k * 16:(k + 1) * 16, at] = piece
                wide = wide[:8]
                for q in range(chips):
                    holder = ((q // 2 * 2 + core) * n_dev + z * 2 + q % 2) * rows
                    peer_signs[r, q, :, at] = sign_of(wide & holder, all_bits)

    def halves(k):
        high, mid = split2(slabs[k].reshape(band, rows))
        return jnp.concatenate([high, mid], axis=0)

    def partial(left, r):
        product = jnp.dot(left, signs[r], preferred_element_type=f32)
        product = product[:band] + product[band:]
        total = None
        for q in range(chips):
            term = product[q * mine:(q + 1) * mine] * peer_signs[r, q]
            total = term if total is None else total + term
        return total

    def settle(k):
        swaps[k].wait_recv()
        for i, d in enumerate(order):
            at = slice(i * picks, (i + 1) * picks)
            part[k, i] = part[k, i] + borrowed[k, :, at]
            if d:
                copy = remote(
                    part.at[k, i], blocks.at[k, i], z_send.at[k, i], z_recv.at[k, i], along(d)
                )
                copy.start()
                passed.append(copy)

    for k in range(chunks):
        for copy in sent[k * len(plane):(k + 1) * len(plane)]:
            copy.wait_recv()
        left = halves(k)
        lent[k] = partial(left, 0)
        copy = remote(lent.at[k], borrowed.at[k], c_send.at[k], c_recv.at[k], sibling)
        copy.start()
        swaps.append(copy)
        if k:
            settle(k - 1)
        mixture = partial(left, 1)
        for i in range(n_z):
            part[k, i] = mixture[:, i * picks:(i + 1) * picks]
    settle(chunks - 1)
    for k in range(chunks):
        total = part[k, n_z - 1]
        for i, copy in enumerate(passed[k * (n_z - 1):(k + 1) * (n_z - 1)]):
            copy.wait_recv()
            total = total + blocks[k, i]
        mixed[k] = total * (1.0 / math.sqrt(rows * n_grp * n_dev))
        for m, at in enumerate(plane):
            copy = remote(
                mixed.at[k], cols.at[k, me], out_send.at[k, m], out_recv.at[k, m], across(*at)[0]
            )
            copy.start()
            given.append(copy)
        cols[k, me] = mixed[k]

    right, held = None, None
    for k in range(chunks):
        for copy in given[k * len(plane):(k + 1) * len(plane)]:
            copy.wait_recv()
        high, mid = split2(cols[k].reshape(band, picks))
        fresh = jnp.concatenate([high, high, mid], axis=1)
        right = fresh if right is None else jnp.concatenate([right, fresh], axis=0)
        gram = lax.dot_general(
            jnp.concatenate([high, mid, high], axis=1), right,
            (((1,), (1,)), ((), ())), preferred_element_type=f32,
        ) * (1.0 / samples)
        if k == 0:
            held = gram
            continue
        if k == 1:
            gram = jnp.concatenate([gram, held], axis=1)
        room = width - gram.shape[1]
        if room:
            gram = jnp.concatenate([gram, jnp.zeros((band, room), f32)], axis=1)
        gram_out[k - 1] = gram
        for i, d in enumerate(order[:-1]):
            copy = remote(
                gram_out.at[k - 1], gram_in.at[k - 1, i], g_send.at[k - 1, i], g_recv.at[k - 1, i], along(d)
            )
            copy.start()
            around.append(copy)

    block = cols[:, :, :, pl.ds(pl.multiple_of(y * LANES, LANES), LANES)].reshape(width, LANES)
    turn_back[...] = jnp.transpose(block)
    sketch_ref[...] = turn_back[pl.ds(pl.multiple_of(x * own, own), own), :]
    for k in range(chunks - 1):
        total = gram_out[k]
        for i, copy in enumerate(around[k * (n_z - 1):(k + 1) * (n_z - 1)]):
            copy.wait_recv()
            total = total + gram_in[k, i]
        gram_sum[k] = total
        copy = remote(gram_sum.at[k], gram_far.at[k], h_send.at[k], h_recv.at[k], sibling)
        copy.start()
        last.append(copy)
    for k, copy in enumerate(last):
        copy.wait_recv()
        total = gram_sum[k] + gram_far[k]
        lower[(k + 1) * band:(k + 2) * band, :] = total
        if k == 0:
            lower[:band, :] = pltpu.roll(total, width - 2 * band, 1)
    full = lower[...]
    row = lax.broadcasted_iota(jnp.int32, (width, width), 0) // band
    col = lax.broadcasted_iota(jnp.int32, (width, width), 1) // band
    gram_ref[...] = jnp.where(col <= row, full, jnp.transpose(full))
    for copy in sent + swaps + passed + given + around + last:
        copy.wait_send()


def general(matrix, flip_bits, sample_rows):
    rows, width = matrix.shape
    n_grp, n_dev = lax.axis_size("grp"), lax.axis_size("dev")
    devices = n_grp * n_dev
    samples = sample_rows.shape[0]
    own = samples // devices
    groups = devices // 4
    chunks = min(width // 8, devices // 2)
    chunk = width // chunks
    pieces = 4
    f32, i32 = jnp.float32, jnp.int32
    dma = pltpu.SemaphoreType.DMA
    vmem = pl.BlockSpec(memory_space=pltpu.VMEM)
    return pl.pallas_call(
        functools.partial(kernel, n_grp, n_dev, rows, own),
        out_shape=(
            pltpu.VMEM((own, width), f32),
            pltpu.VMEM((width, width), f32),
        ),
        in_specs=[pl.BlockSpec(memory_space=pl.ANY)] * 3,
        out_specs=(vmem, vmem),
        scratch_shapes=[
            pltpu.VMEM((rows // LANES, LANES), i32),
            pltpu.VMEM((samples // LANES, LANES), i32),
            pltpu.VMEM((rows, width), f32),
            pltpu.VMEM((2, 4, rows // 2, width), f32),
            pltpu.VMEM((3, rows // LANES, LANES), i32),
            pltpu.VMEM((samples // 2, LANES), i32),
            pltpu.VMEM((groups * own, LANES), i32),
            pltpu.VMEM((groups * own, rows), jnp.bfloat16),
            pltpu.VMEM((2, groups, own // 2, width), f32),
            pltpu.VMEM((2, groups, own // 2, width), f32),
            pltpu.VMEM((chunks, chunk, width), f32),
            pltpu.VMEM((devices, chunk, width), f32),
            pltpu.VMEM((chunks, chunk, width), f32),
            pltpu.VMEM((chunk, width), f32),
            dma((3,)), dma((2,)), dma((2,)), dma((pieces,)), dma((pieces,)), dma((pieces,)), dma((pieces,)),
            dma((3,)), dma((3,)), dma((2,)), dma((2,)), dma, dma, dma, dma,
            pltpu.SemaphoreType.REGULAR((16,)),
        ],
        compiler_params=pltpu.CompilerParams(collective_id=0, has_side_effects=True),
    )(
        matrix,
        flip_bits.reshape(rows // LANES, LANES),
        sample_rows.reshape(samples // LANES, LANES),
    )


def plane_body(matrix, flip_bits, sample_rows):
    rows, width = matrix.shape
    n_grp, n_dev = lax.axis_size("grp"), lax.axis_size("dev")
    samples = sample_rows.shape[0]
    own = samples // (n_grp * n_dev)
    n_y, n_z, chips = n_grp // 2, n_dev // 2, n_grp
    mine = 8
    chunks, band, picks = width // (chips * mine), chips * mine, n_y * LANES
    f32, i32, bf16 = jnp.float32, jnp.int32, jnp.bfloat16
    dma = pltpu.SemaphoreType.DMA
    vmem = pl.BlockSpec(memory_space=pltpu.VMEM)
    return pl.pallas_call(
        functools.partial(plane_kernel, n_grp, n_dev, rows, own),
        out_shape=(pltpu.VMEM((own, width), f32), pltpu.VMEM((width, width), f32)),
        in_specs=[pl.BlockSpec(memory_space=pl.ANY)] * 3,
        out_specs=(vmem, vmem),
        scratch_shapes=[
            pltpu.VMEM((rows, width), f32),
            pltpu.VMEM((rows // LANES, LANES), i32),
            pltpu.VMEM((samples // LANES, LANES), i32),
            pltpu.VMEM((width, rows), f32),
            pltpu.VMEM((chunks, chips, mine, rows), f32),
            pltpu.VMEM((2, rows, n_z * picks), bf16),
            pltpu.VMEM((2, chips, mine, n_z * picks), f32),
            pltpu.VMEM((chunks, mine, n_z * picks), f32),
            pltpu.VMEM((chunks, mine, n_z * picks), f32),
            pltpu.VMEM((chunks, n_z, mine, picks), f32),
            pltpu.VMEM((chunks, n_z - 1, mine, picks), f32),
            pltpu.VMEM((chunks, mine, picks), f32),
            pltpu.VMEM((chunks, chips, mine, picks), f32),
            pltpu.VMEM((LANES, width), f32),
            pltpu.VMEM((chunks - 1, band, width), f32),
            pltpu.VMEM((chunks - 1, n_z - 1, band, width), f32),
            pltpu.VMEM((chunks - 1, band, width), f32),
            pltpu.VMEM((chunks - 1, band, width), f32),
            pltpu.VMEM((width, width), f32),
            dma((3,)), dma((chunks, chips - 1)), dma((chunks, chips - 1)), dma((chunks,)), dma((chunks,)),
            dma((chunks, n_z - 1)), dma((chunks, n_z - 1)), dma((chunks, chips - 1)), dma((chunks, chips - 1)),
            dma((chunks - 1, n_z - 1)), dma((chunks - 1, n_z - 1)), dma((chunks - 1,)), dma((chunks - 1,)),
        ],
        compiler_params=pltpu.CompilerParams(collective_id=0, has_side_effects=True),
    )(
        matrix,
        flip_bits.reshape(rows // LANES, LANES),
        sample_rows.reshape(samples // LANES, LANES),
    )


def body(matrix, flip_bits, sample_rows):
    rows, width = matrix.shape
    n_grp, n_dev = lax.axis_size("grp"), lax.axis_size("dev")
    paired = sample_rows.shape[0] * 2 == n_grp * n_dev * LANES
    tiled = width == LANES and width % (n_grp * 8) == 0 and width // (n_grp * 8) >= 3
    if paired and tiled and rows % LANES == 0:
        return plane_body(matrix, flip_bits, sample_rows)
    return general(matrix, flip_bits, sample_rows)


def solution(mesh):
    return jax.shard_map(
        body,
        mesh=mesh,
        in_specs=(P(("grp", "dev"), None), P(("grp", "dev")), P()),
        out_specs=(P(("grp", "dev"), None), P()),
        check_vma=False,
    )
```

```python
import functools
import math

import jax
import jax.numpy as jnp
from jax import lax
from jax.experimental import pallas as pl
from jax.experimental.pallas import tpu as pltpu
from jax.sharding import PartitionSpec as P

MESH = pl.DeviceIdType.MESH
LANES = 128


def loop(count, fn):
    if count <= 8:
        for step in range(count):
            fn(step)
    else:
        lax.fori_loop(0, count, lambda step, carry: (fn(step), carry)[1], 0)


def parity(bits, width):
    shift = 1
    while shift * 2 < width:
        shift *= 2
    while shift:
        bits = bits ^ (bits >> shift)
        shift //= 2
    return bits & 1


def sign_of(bits, width):
    return (1 - 2 * parity(bits, width)).astype(jnp.float32)


def split3(value):
    high = value.astype(jnp.bfloat16)
    rest = value - high.astype(jnp.float32)
    mid = rest.astype(jnp.bfloat16)
    low = (rest - mid.astype(jnp.float32)).astype(jnp.bfloat16)
    return high, mid, low


def kernel(
    n_grp, n_dev, rows, own,
    x_ref, flip_hbm, sample_hbm, sketch_ref, gram_ref,
    flip_ref, sample_ref, x_full, slabs, flips, cols, index, base, part, blocks, gpart, gslots, gfull, reduced,
    load_sem, pair_send, pair_recv, twin_send, twin_recv, fwd_send, fwd_recv,
    flip_send, flip_recv, rs_send, rs_recv, g_send, g_recv, b_send, b_recv,
    ready,
):
    f32 = jnp.float32
    devices = n_grp * n_dev
    n_y, n_z = n_grp // 2, n_dev // 2
    groups = n_y * n_z
    width = x_ref.shape[1]
    pieces = twin_send.shape[0]
    piece = rows // pieces
    samples = sample_hbm.shape[0] * LANES
    row_bits = rows.bit_length() - 1
    all_bits = (rows * devices).bit_length() - 1
    me_g, me_d = lax.axis_index("grp"), lax.axis_index("dev")
    core, y = lax.rem(me_g, 2), lax.div(me_g, 2)
    x, z = lax.rem(me_d, 2), lax.div(me_d, 2)
    pair_g = me_g + 1 - 2 * core
    twin_d = me_d + 1 - 2 * x
    mine = y * n_z + z

    def remote(src, dst, send, recv, grp, dev):
        return pltpu.make_async_remote_copy(
            src_ref=src, dst_ref=dst, send_sem=send, recv_sem=recv,
            device_id=(grp, dev), device_id_type=MESH,
        )

    barrier = pltpu.get_barrier_semaphore()

    def signal(sem, grp, dev):
        pl.semaphore_signal(sem, inc=1, device_id=(grp, dev), device_id_type=MESH)

    def along_y(step):
        return me_g + 2 * step, me_d

    def along_z(step):
        return me_g, me_d + 2 * step

    def tell_line(sem, at, size, reach, along):
        for step in range(1, min(reach, size - 1) + 1):
            @pl.when(at >= step)
            def _():
                signal(sem, *along(-step))

            @pl.when(at + step < size)
            def _():
                signal(sem, *along(step))

    def line_count(at, size, reach):
        return jnp.minimum(at, reach) + jnp.minimum(size - 1 - at, reach)

    signal(barrier, pair_g, me_d)
    signal(barrier, me_g, twin_d)
    tell_line(barrier, y, n_y, 1, along_y)
    tell_line(barrier, z, n_z, 1, along_z)

    loads = [
        pltpu.make_async_copy(sample_hbm, sample_ref, load_sem.at[0]),
        pltpu.make_async_copy(flip_hbm, flip_ref, load_sem.at[1]),
        pltpu.make_async_copy(x_ref, x_full, load_sem.at[2]),
    ]
    for copy in loads:
        copy.start()
    pl.semaphore_wait(barrier, 2 + line_count(y, n_y, 1) + line_count(z, n_z, 1))

    rounds = []
    for at, size, along in ((z, n_z, along_z), (y, n_y, along_y)):
        reach = 1
        while reach < size - 1:
            rounds.append((at, size, reach, along))
            reach *= 2
    rounds.append((y, n_y, n_y - 1, along_y))

    def open_round(k):
        if k < len(rounds):
            at, size, reach, along = rounds[k]
            tell_line(ready.at[k], at, size, reach, along)
        elif k == len(rounds):
            signal(ready.at[k], me_g, twin_d)
        else:
            signal(ready.at[k], pair_g, me_d)

    def close_round(k):
        if k < len(rounds):
            at, size, reach, along = rounds[k]
            pl.semaphore_wait(ready.at[k], line_count(at, size, reach))
        else:
            pl.semaphore_wait(ready.at[k], 1)

    half = width // 2
    left = lax.broadcasted_iota(jnp.int32, (1, width), 1) < half

    def swap(value):
        return pltpu.roll(value, half, value.ndim - 1)

    for copy in loads:
        copy.wait()
    top, bottom = x_full[pl.ds(0, rows // 2), :], x_full[pl.ds(rows // 2, rows // 2), :]
    slabs[0, 0] = jnp.where(left, top, swap(bottom))
    slabs[1, 0] = jnp.where(left, swap(top), bottom)
    twin, pair = [], []
    for h in range(2):
        for c in range(pieces // 2):
            at = pl.ds(c * piece, piece)
            k = h * (pieces // 2) + c
            copy = remote(
                slabs.at[h, 0, at], slabs.at[h, 2, at],
                twin_send.at[k], twin_recv.at[k], me_g, twin_d,
            )
            copy.start()
            twin.append(copy)
    for h in range(2):
        copy = remote(
            slabs.at[h, 0], slabs.at[h, 1], pair_send.at[h], pair_recv.at[h], pair_g, me_d
        )
        copy.start()
        pair.append(copy)
    flip_copies = [
        remote(flip_ref, flips.at[0], flip_send.at[0], flip_recv.at[0], pair_g, me_d),
        remote(flip_ref, flips.at[1], flip_send.at[1], flip_recv.at[1], me_g, twin_d),
        remote(flips.at[1], flips.at[2], flip_send.at[2], flip_recv.at[2], pair_g, me_d),
    ]
    open_round(0)
    for copy in flip_copies[:2]:
        copy.start()

    span = n_dev * own // LANES
    for i in range(n_y):
        for r in range(span):
            line = sample_ref[pl.ds((i * 2 + core) * span + r, 1), :]
            cols[pl.ds((i * span + r) * LANES, LANES), :] = jnp.transpose(
                jnp.broadcast_to(line, (LANES, LANES))
            )
    for i in range(n_y):
        for j in range(n_z):
            index[pl.ds((i * n_z + j) * own, own), :] = cols[
                pl.ds((i * n_dev + j * 2 + x) * own, own), :
            ]
    close_round(0)
    open_round(1)
    picks = groups * own
    wanted = index[...]
    for k in range(rows // LANES):
        lane = lax.broadcasted_iota(jnp.int32, (picks, LANES), 1) + k * LANES
        base[:, k * LANES:(k + 1) * LANES] = sign_of(wanted & lane, row_bits).astype(jnp.bfloat16)

    owner_signs = [
        sign_of(wanted & ((grp * n_dev + dev) * rows), all_bits)
        for grp, dev in ((me_g, me_d), (pair_g, me_d), (me_g, twin_d), (pair_g, twin_d))
    ]

    def term(h, slot, flip_bits, grp, dev):
        signs = base[...]
        toggles = (1 - 2 * flip_bits).astype(f32).astype(jnp.bfloat16)
        signs = jnp.concatenate(
            [
                signs[:, k * LANES:(k + 1) * LANES] * toggles[k:k + 1, :]
                for k in range(rows // LANES)
            ],
            axis=1,
        )
        packed = slabs[h, slot]
        high, mid, low = split3(packed)
        high_s, mid_s, low_s = split3(swap(packed))
        right = jnp.concatenate(
            [
                jnp.concatenate([jnp.where(left, high, mid_s), low], axis=1),
                jnp.concatenate([jnp.where(left, high_s, mid), low_s], axis=1),
            ],
            axis=0,
        )
        product = jnp.dot(signs, right, preferred_element_type=f32)
        first, last = product[:, :width], product[:, width:]
        return (first + swap(first) + last) * owner_signs[slot]

    def give(h, i, j):
        to_y, to_z = lax.rem(y + i, n_y), lax.rem(z + j, n_z)
        remote(
            part.at[h, to_y * n_z + to_z], blocks.at[h, mine], rs_send.at[h], rs_recv.at[h],
            to_y * 2 + core, to_z * 2 + x,
        ).start()

    for k in range(1, len(rounds) - 1):
        close_round(k)
        open_round(k + 1)
    totals = [term(h, 0, flip_ref[...], me_g, me_d) for h in range(2)]
    close_round(len(rounds) - 1)
    open_round(len(rounds))
    flip_copies[0].wait_recv()
    for h in range(2):
        pair[h].wait_recv()
        totals[h] = totals[h] + term(h, 1, flips[0], pair_g, me_d)
    flip_copies[1].wait_recv()
    flip_copies[2].start()
    forward = []
    for h in range(2):
        for c in range(pieces // 2):
            at = pl.ds(c * piece, piece)
            k = h * (pieces // 2) + c
            twin[k].wait_recv()
            copy = remote(
                slabs.at[h, 2, at], slabs.at[h, 3, at],
                fwd_send.at[k], fwd_recv.at[k], pair_g, me_d,
            )
            copy.start()
            forward.append(copy)
        total = totals[h] + term(h, 2, flips[1], me_g, twin_d)
        if h == 0:
            flip_copies[2].wait_recv()
        for copy in forward[h * (pieces // 2):]:
            copy.wait_recv()
        total = total + term(h, 3, flips[2], pair_g, twin_d)
        total = total.reshape(groups, own, width)
        part[h] = jnp.where(
            left.reshape(1, 1, width), total[:, :own // 2], swap(total[:, own // 2:])
        )
        if h == 0:
            close_round(len(rounds))
            open_round(len(rounds) + 1)
        for i in range(n_y - 1, -1, -1):
            loop(n_z - (i == 0), lambda j: give(h, i, j + (i == 0)))
        blocks[h, mine] = part[h, mine]
    sums = []
    for h in range(2):
        others = blocks.at[h, pl.ds(0, groups - 1)]
        pltpu.make_async_copy(others, others, rs_recv.at[h]).wait()
        summed = blocks[h, 0]
        for i in range(1, groups):
            summed = summed + blocks[h, i]
        sums.append(summed)
    sketch = jnp.concatenate(
        [
            jnp.where(left, sums[0], swap(sums[1])),
            jnp.where(left, swap(sums[0]), sums[1]),
        ],
        axis=0,
    )
    sketch = sketch * (1.0 / math.sqrt(rows * devices))
    sketch_ref[...] = sketch

    close_round(len(rounds) + 1)
    chunks = gfull.shape[0]
    across = min(chunks, n_dev // 2)
    first = (n_dev - across) // 2
    chunk = width // chunks
    linear = me_g * n_dev + me_d
    reducer = (me_g < chunks // across) & (me_d >= first) & (me_d < first + across)
    my_chunk = me_g * across + me_d - first
    gram = lax.dot_general(
        sketch, sketch, (((0,), (0,)), ((), ())),
        precision=lax.Precision.HIGHEST, preferred_element_type=f32,
    )
    gpart[...] = gram.reshape(chunks, chunk, width)
    turn = lax.rem(linear, chunks)
    for k in range(chunks):
        to = lax.rem(k + turn, chunks)
        to_g, to_d = lax.div(to, across), first + lax.rem(to, across)

        @pl.when((me_g != to_g) | (me_d != to_d))
        def _():
            remote(gpart.at[to], gslots.at[linear], g_send, g_recv, to_g, to_d).start()

    @pl.when(reducer)
    def _():
        gslots[linear] = gpart[my_chunk]
        rest = gslots.at[pl.ds(0, devices - 1)]
        pltpu.make_async_copy(rest, rest, g_recv).wait()
        result = jnp.sum(gslots[...], axis=0) * (1.0 / samples)
        reduced[...] = result
        gfull[my_chunk] = result

        def tell(i, j):
            remote(
                reduced, gfull.at[my_chunk], b_send, b_recv,
                lax.rem(me_g + i, n_grp), lax.rem(me_d + j, n_dev),
            ).start()

        for i in range(n_grp - 1, -1, -1):
            loop(n_dev - (i == 0), lambda j: tell(i, j + (i == 0)))
        most = gfull.at[pl.ds(0, chunks - 1)]
        pltpu.make_async_copy(most, most, b_recv).wait()
        pltpu.make_async_copy(rest, rest, b_send).wait()
        pltpu.make_async_copy(most, most, g_send).wait()

    @pl.when(jnp.logical_not(reducer))
    def _():
        pltpu.make_async_copy(gfull, gfull, b_recv).wait()
        pltpu.make_async_copy(gfull, gfull, g_send).wait()

    gram_ref[...] = gfull[...].reshape(width, width)
    for copy in twin + forward + flip_copies + pair:
        copy.wait_send()
    for h in range(2):
        others = blocks.at[h, pl.ds(0, groups - 1)]
        pltpu.make_async_copy(others, others, rs_send.at[h]).wait()


def split2(value):
    high = value.astype(jnp.bfloat16)
    return high, (value - high.astype(jnp.float32)).astype(jnp.bfloat16)


def plane_kernel(
    n_grp, n_dev, rows, own,
    x_hbm, flip_hbm, sample_hbm, sketch_ref, gram_ref,
    x_ref, flip_ref, sample_ref, turned, slabs, signs, peer_signs, part, blocks, mixed, cols, turn_back,
    gpart, gslots, ghalf, gmine, gfull,
    load_sem, in_send, in_recv, z_send, z_recv, out_send, out_recv, core_send, core_recv, gz_send, gz_recv, far_recv,
):
    f32, bf16 = jnp.float32, jnp.bfloat16
    width = x_ref.shape[1]
    n_y, n_z = n_grp // 2, n_dev // 2
    peers = n_grp * 2
    mine = width // peers
    span = n_dev * own // LANES
    samples = sample_ref.shape[0] * LANES
    picks = n_grp * LANES
    row_bits = rows.bit_length() - 1
    all_bits = (rows * n_grp * n_dev).bit_length() - 1
    me_g, me_d = lax.axis_index("grp"), lax.axis_index("dev")
    core, y = lax.rem(me_g, 2), lax.div(me_g, 2)
    x, z = lax.rem(me_d, 2), lax.div(me_d, 2)
    me = me_g * 2 + x

    plane = [(a, k, b) for a in range(n_y) for k in range(2) for b in range(2)][:0:-1]
    plane = sorted(plane, key=lambda at: -((at[0] > 0) + at[1]))

    def peer(a, k, b):
        to_y, to_x, to_c = lax.rem(y + a, n_y), lax.rem(x + k, 2), lax.rem(core + b, 2)
        return to_y * 2 + to_c, to_x, to_c

    far, first, final = [], 0, n_z - 1
    for _ in range(n_z - 1):
        down = z - first >= final - z
        far.append(jnp.where(down, first, final))
        first, final = first + jnp.where(down, 1, 0), final - jnp.where(down, 0, 1)
    others = [lax.rem(z + d, n_z) for d in range(1, n_z)]

    def remote(src, dst, send, recv, grp, dev):
        return pltpu.make_async_remote_copy(
            src_ref=src, dst_ref=dst, send_sem=send, recv_sem=recv,
            device_id=(grp, dev), device_id_type=MESH,
        )

    def arrival(slot, sem):
        pltpu.make_async_copy(slot, slot, sem).wait()

    barrier = pltpu.get_barrier_semaphore()
    loads = [
        pltpu.make_async_copy(x_hbm, x_ref, load_sem.at[0]),
        pltpu.make_async_copy(flip_hbm, flip_ref, load_sem.at[1]),
        pltpu.make_async_copy(sample_hbm, sample_ref, load_sem.at[2]),
    ]
    for at in plane:
        grp, to_x, _ = peer(*at)
        pl.semaphore_signal(barrier, inc=1, device_id=(grp, z * 2 + to_x), device_id_type=MESH)
    for d in range(1, n_z):
        pl.semaphore_signal(
            barrier, inc=1, device_id=(me_g, lax.rem(z + d, n_z) * 2 + x), device_id_type=MESH
        )
    for copy in loads:
        copy.start()
    for copy in loads:
        copy.wait()

    toggles = (1 - 2 * flip_ref[...]).astype(f32)
    for k in range(rows // LANES):
        at = slice(k * LANES, (k + 1) * LANES)
        turned[:, at] = jnp.transpose(x_ref[at, :]) * toggles[k:k + 1, :]
    pl.semaphore_wait(barrier, peers - 1 + n_z - 1)

    sent = []
    for m, at in enumerate(plane):
        grp, to_x, _ = peer(*at)
        to = grp * 2 + to_x
        copy = remote(
            turned.at[pl.ds(pl.multiple_of(to * mine, mine), mine)], slabs.at[me],
            in_send.at[m], in_recv.at[m], grp, z * 2 + to_x,
        )
        copy.start()
        sent.append(copy)
    slabs[me] = turned[pl.ds(pl.multiple_of(me * mine, mine), mine), :]

    low = lax.broadcasted_iota(jnp.int32, (16, LANES), 0)
    for i, to_z in enumerate(far + [z]):
        for g in range(n_grp):
            wanted = sample_ref[pl.ds(g * span + to_z, 1), :]
            wide = jnp.broadcast_to(wanted, (16, LANES))
            pieces = [sign_of(wide & low, 16).astype(bf16)]
            for bit in range(4, row_bits):
                factor = (1 - 2 * ((wide >> bit) & 1)).astype(f32).astype(bf16)
                pieces += [piece * factor for piece in pieces]
            for k, piece in enumerate(pieces):
                signs[i, k * 16:(k + 1) * 16, g * LANES:(g + 1) * LANES] = piece
            wide = wide[:8]
            for p in range(peers):
                holder = ((p // 2) * n_dev + z * 2 + p % 2) * rows
                peer_signs[i, p, :, g * LANES:(g + 1) * LANES] = sign_of(wide & holder, all_bits)

    for copy in sent:
        copy.wait_recv()
    high, mid = split2(slabs[...].reshape(peers * mine, rows))
    left = jnp.concatenate([high, mid], axis=0)
    passed = []
    for i, to_z in enumerate(far + [z]):
        product = jnp.dot(left, signs[i], preferred_element_type=f32)
        product = product[:peers * mine] + product[peers * mine:]
        total = None
        for p in range(peers):
            term = product[p * mine:(p + 1) * mine].reshape(mine // 8, 8, picks) * peer_signs[i, p][None]
            total = term if total is None else total + term
        part[i] = total.reshape(mine, picks)
        if i < n_z - 1:
            copy = remote(
                part.at[i], blocks.at[z], z_send.at[i], z_recv.at[z], me_g, to_z * 2 + x
            )
            copy.start()
            passed.append(copy)
    total = part[n_z - 1]
    for from_z in others:
        arrival(blocks.at[from_z], z_recv.at[from_z])
        total = total + blocks[from_z]
    total = total * (1.0 / math.sqrt(rows * n_grp * n_dev))
    for c in range(2):
        mixed[c] = jnp.concatenate(
            [total[:, g * LANES:(g + 1) * LANES] for g in range(c, n_grp, 2)], axis=1
        )
    given = []
    for m, at in enumerate(plane):
        grp, to_x, to_c = peer(*at)
        copy = remote(
            mixed.at[to_c], cols.at[me], out_send.at[m], out_recv.at[m], grp, z * 2 + to_x
        )
        copy.start()
        given.append(copy)
    cols[me] = mixed[core]
    for copy in given:
        copy.wait_recv()

    held = cols[...].reshape(width, n_y * LANES)
    high, mid = split2(held)
    gram = lax.dot_general(
        jnp.concatenate([high, mid, high], axis=1), jnp.concatenate([high, high, mid], axis=1),
        (((1,), (1,)), ((), ())), preferred_element_type=f32,
    )
    half = width // 2
    gpart[...] = (gram * (1.0 / samples)).reshape(2, half, width)
    sibling = me_g + 1 - 2 * core
    swap = remote(gpart.at[1 - core], gslots, core_send.at[0], core_recv.at[0], sibling, me_d)
    swap.start()
    block = cols[:, :, pl.ds(pl.multiple_of(y * LANES, LANES), LANES)].reshape(width, LANES)
    turn_back[...] = jnp.transpose(block)
    sketch_ref[...] = turn_back[pl.ds(pl.multiple_of(x * own, own), own), :]
    swap.wait_recv()
    gmine[...] = gpart[core] + gslots[...]
    told = [
        remote(gfull.at[core], gfull.at[core], gz_send.at[d - 1], far_recv.at[0], me_g, d * 2 + x)
        for d in range(n_z - 1, 0, -1)
    ]
    last = remote(gfull.at[core], gfull.at[core], core_send.at[1], core_recv.at[1], sibling, me_d)
    report = remote(gmine, ghalf.at[z], gz_send.at[0], gz_recv.at[z], me_g, x)

    @pl.when(z == 0)
    def _():
        result = gmine[...]
        for d in range(1, n_z):
            arrival(ghalf.at[d], gz_recv.at[d])
            result = result + ghalf[d]
        gfull[core] = result
        last.start()
        for copy in told:
            copy.start()
        for copy in told:
            copy.wait_send()

    @pl.when(z > 0)
    def _():
        report.start()
        arrival(gfull.at[core], far_recv.at[0])
        last.start()
        report.wait_send()

    last.wait_recv()
    gram_ref[...] = gfull[...].reshape(width, width)
    for copy in sent + passed + given + [swap, last]:
        copy.wait_send()


def general(matrix, flip_bits, sample_rows):
    rows, width = matrix.shape
    n_grp, n_dev = lax.axis_size("grp"), lax.axis_size("dev")
    devices = n_grp * n_dev
    samples = sample_rows.shape[0]
    own = samples // devices
    groups = devices // 4
    chunks = min(width // 8, devices // 2)
    chunk = width // chunks
    pieces = 4
    f32, i32 = jnp.float32, jnp.int32
    dma = pltpu.SemaphoreType.DMA
    vmem = pl.BlockSpec(memory_space=pltpu.VMEM)
    return pl.pallas_call(
        functools.partial(kernel, n_grp, n_dev, rows, own),
        out_shape=(
            pltpu.VMEM((own, width), f32),
            pltpu.VMEM((width, width), f32),
        ),
        in_specs=[pl.BlockSpec(memory_space=pl.ANY)] * 3,
        out_specs=(vmem, vmem),
        scratch_shapes=[
            pltpu.VMEM((rows // LANES, LANES), i32),
            pltpu.VMEM((samples // LANES, LANES), i32),
            pltpu.VMEM((rows, width), f32),
            pltpu.VMEM((2, 4, rows // 2, width), f32),
            pltpu.VMEM((3, rows // LANES, LANES), i32),
            pltpu.VMEM((samples // 2, LANES), i32),
            pltpu.VMEM((groups * own, LANES), i32),
            pltpu.VMEM((groups * own, rows), jnp.bfloat16),
            pltpu.VMEM((2, groups, own // 2, width), f32),
            pltpu.VMEM((2, groups, own // 2, width), f32),
            pltpu.VMEM((chunks, chunk, width), f32),
            pltpu.VMEM((devices, chunk, width), f32),
            pltpu.VMEM((chunks, chunk, width), f32),
            pltpu.VMEM((chunk, width), f32),
            dma((3,)), dma((2,)), dma((2,)), dma((pieces,)), dma((pieces,)), dma((pieces,)), dma((pieces,)),
            dma((3,)), dma((3,)), dma((2,)), dma((2,)), dma, dma, dma, dma,
            pltpu.SemaphoreType.REGULAR((16,)),
        ],
        compiler_params=pltpu.CompilerParams(collective_id=0, has_side_effects=True),
    )(
        matrix,
        flip_bits.reshape(rows // LANES, LANES),
        sample_rows.reshape(samples // LANES, LANES),
    )


def plane_body(matrix, flip_bits, sample_rows):
    rows, width = matrix.shape
    n_grp, n_dev = lax.axis_size("grp"), lax.axis_size("dev")
    samples = sample_rows.shape[0]
    own = samples // (n_grp * n_dev)
    n_y, n_z, peers = n_grp // 2, n_dev // 2, n_grp * 2
    mine, picks, half = width // peers, n_grp * LANES, width // 2
    f32, i32, bf16 = jnp.float32, jnp.int32, jnp.bfloat16
    dma = pltpu.SemaphoreType.DMA
    vmem = pl.BlockSpec(memory_space=pltpu.VMEM)
    return pl.pallas_call(
        functools.partial(plane_kernel, n_grp, n_dev, rows, own),
        out_shape=(pltpu.VMEM((own, width), f32), pltpu.VMEM((width, width), f32)),
        in_specs=[pl.BlockSpec(memory_space=pl.ANY)] * 3,
        out_specs=(vmem, vmem),
        scratch_shapes=[
            pltpu.VMEM((rows, width), f32),
            pltpu.VMEM((rows // LANES, LANES), i32),
            pltpu.VMEM((samples // LANES, LANES), i32),
            pltpu.VMEM((width, rows), f32),
            pltpu.VMEM((peers, mine, rows), f32),
            pltpu.VMEM((n_z, rows, picks), bf16),
            pltpu.VMEM((n_z, peers, 8, picks), f32),
            pltpu.VMEM((n_z, mine, picks), f32),
            pltpu.VMEM((n_z, mine, picks), f32),
            pltpu.VMEM((2, mine, n_y * LANES), f32),
            pltpu.VMEM((peers, mine, n_y * LANES), f32),
            pltpu.VMEM((LANES, width), f32),
            pltpu.VMEM((2, half, width), f32),
            pltpu.VMEM((half, width), f32),
            pltpu.VMEM((n_z, half, width), f32),
            pltpu.VMEM((half, width), f32),
            pltpu.VMEM((2, half, width), f32),
            dma((3,)), dma((peers - 1,)), dma((peers - 1,)), dma((n_z - 1,)), dma((n_z,)),
            dma((peers - 1,)), dma((peers - 1,)), dma((2,)), dma((2,)), dma((n_z - 1,)), dma((n_z,)), dma((1,)),
        ],
        compiler_params=pltpu.CompilerParams(collective_id=0, has_side_effects=True),
    )(
        matrix,
        flip_bits.reshape(rows // LANES, LANES),
        sample_rows.reshape(samples // LANES, LANES),
    )


def body(matrix, flip_bits, sample_rows):
    rows, width = matrix.shape
    n_grp, n_dev = lax.axis_size("grp"), lax.axis_size("dev")
    paired = sample_rows.shape[0] * 2 == n_grp * n_dev * LANES
    tiled = width == LANES and width % (n_grp * 2 * 8) == 0
    if paired and tiled and rows % LANES == 0:
        return plane_body(matrix, flip_bits, sample_rows)
    return general(matrix, flip_bits, sample_rows)


def solution(mesh):
    return jax.shard_map(
        body,
        mesh=mesh,
        in_specs=(P(("grp", "dev"), None), P(("grp", "dev")), P()),
        out_specs=(P(("grp", "dev"), None), P()),
        check_vma=False,
    )
```

```python
import functools
import math

import jax
import jax.numpy as jnp
from jax import lax
from jax.experimental import pallas as pl
from jax.experimental.pallas import tpu as pltpu
from jax.sharding import PartitionSpec as P

MESH = pl.DeviceIdType.MESH
LANES = 128


def loop(count, fn):
    if count <= 8:
        for step in range(count):
            fn(step)
    else:
        lax.fori_loop(0, count, lambda step, carry: (fn(step), carry)[1], 0)


def parity(bits, width):
    shift = 1
    while shift * 2 < width:
        shift *= 2
    while shift:
        bits = bits ^ (bits >> shift)
        shift //= 2
    return bits & 1


def sign_of(bits, width):
    return (1 - 2 * parity(bits, width)).astype(jnp.float32)


def split3(value):
    high = value.astype(jnp.bfloat16)
    rest = value - high.astype(jnp.float32)
    mid = rest.astype(jnp.bfloat16)
    low = (rest - mid.astype(jnp.float32)).astype(jnp.bfloat16)
    return high, mid, low


def kernel(
    n_grp, n_dev, rows, own,
    x_ref, flip_hbm, sample_hbm, sketch_ref, gram_ref,
    flip_ref, sample_ref, x_full, slabs, flips, cols, index, base, part, blocks, gpart, gslots, gfull, reduced,
    load_sem, pair_send, pair_recv, twin_send, twin_recv, fwd_send, fwd_recv,
    flip_send, flip_recv, rs_send, rs_recv, g_send, g_recv, b_send, b_recv,
    ready,
):
    f32 = jnp.float32
    devices = n_grp * n_dev
    n_y, n_z = n_grp // 2, n_dev // 2
    groups = n_y * n_z
    width = x_ref.shape[1]
    pieces = twin_send.shape[0]
    piece = rows // pieces
    samples = sample_hbm.shape[0] * LANES
    row_bits = rows.bit_length() - 1
    all_bits = (rows * devices).bit_length() - 1
    me_g, me_d = lax.axis_index("grp"), lax.axis_index("dev")
    core, y = lax.rem(me_g, 2), lax.div(me_g, 2)
    x, z = lax.rem(me_d, 2), lax.div(me_d, 2)
    pair_g = me_g + 1 - 2 * core
    twin_d = me_d + 1 - 2 * x
    mine = y * n_z + z

    def remote(src, dst, send, recv, grp, dev):
        return pltpu.make_async_remote_copy(
            src_ref=src, dst_ref=dst, send_sem=send, recv_sem=recv,
            device_id=(grp, dev), device_id_type=MESH,
        )

    barrier = pltpu.get_barrier_semaphore()

    def signal(sem, grp, dev):
        pl.semaphore_signal(sem, inc=1, device_id=(grp, dev), device_id_type=MESH)

    def along_y(step):
        return me_g + 2 * step, me_d

    def along_z(step):
        return me_g, me_d + 2 * step

    def tell_line(sem, at, size, reach, along):
        for step in range(1, min(reach, size - 1) + 1):
            @pl.when(at >= step)
            def _():
                signal(sem, *along(-step))

            @pl.when(at + step < size)
            def _():
                signal(sem, *along(step))

    def line_count(at, size, reach):
        return jnp.minimum(at, reach) + jnp.minimum(size - 1 - at, reach)

    signal(barrier, pair_g, me_d)
    signal(barrier, me_g, twin_d)
    tell_line(barrier, y, n_y, 1, along_y)
    tell_line(barrier, z, n_z, 1, along_z)

    loads = [
        pltpu.make_async_copy(sample_hbm, sample_ref, load_sem.at[0]),
        pltpu.make_async_copy(flip_hbm, flip_ref, load_sem.at[1]),
        pltpu.make_async_copy(x_ref, x_full, load_sem.at[2]),
    ]
    for copy in loads:
        copy.start()
    pl.semaphore_wait(barrier, 2 + line_count(y, n_y, 1) + line_count(z, n_z, 1))

    rounds = []
    for at, size, along in ((z, n_z, along_z), (y, n_y, along_y)):
        reach = 1
        while reach < size - 1:
            rounds.append((at, size, reach, along))
            reach *= 2
    rounds.append((y, n_y, n_y - 1, along_y))

    def open_round(k):
        if k < len(rounds):
            at, size, reach, along = rounds[k]
            tell_line(ready.at[k], at, size, reach, along)
        elif k == len(rounds):
            signal(ready.at[k], me_g, twin_d)
        else:
            signal(ready.at[k], pair_g, me_d)

    def close_round(k):
        if k < len(rounds):
            at, size, reach, along = rounds[k]
            pl.semaphore_wait(ready.at[k], line_count(at, size, reach))
        else:
            pl.semaphore_wait(ready.at[k], 1)

    half = width // 2
    left = lax.broadcasted_iota(jnp.int32, (1, width), 1) < half

    def swap(value):
        return pltpu.roll(value, half, value.ndim - 1)

    for copy in loads:
        copy.wait()
    top, bottom = x_full[pl.ds(0, rows // 2), :], x_full[pl.ds(rows // 2, rows // 2), :]
    slabs[0, 0] = jnp.where(left, top, swap(bottom))
    slabs[1, 0] = jnp.where(left, swap(top), bottom)
    twin, pair = [], []
    for h in range(2):
        for c in range(pieces // 2):
            at = pl.ds(c * piece, piece)
            k = h * (pieces // 2) + c
            copy = remote(
                slabs.at[h, 0, at], slabs.at[h, 2, at],
                twin_send.at[k], twin_recv.at[k], me_g, twin_d,
            )
            copy.start()
            twin.append(copy)
    for h in range(2):
        copy = remote(
            slabs.at[h, 0], slabs.at[h, 1], pair_send.at[h], pair_recv.at[h], pair_g, me_d
        )
        copy.start()
        pair.append(copy)
    flip_copies = [
        remote(flip_ref, flips.at[0], flip_send.at[0], flip_recv.at[0], pair_g, me_d),
        remote(flip_ref, flips.at[1], flip_send.at[1], flip_recv.at[1], me_g, twin_d),
        remote(flips.at[1], flips.at[2], flip_send.at[2], flip_recv.at[2], pair_g, me_d),
    ]
    open_round(0)
    for copy in flip_copies[:2]:
        copy.start()

    span = n_dev * own // LANES
    for i in range(n_y):
        for r in range(span):
            line = sample_ref[pl.ds((i * 2 + core) * span + r, 1), :]
            cols[pl.ds((i * span + r) * LANES, LANES), :] = jnp.transpose(
                jnp.broadcast_to(line, (LANES, LANES))
            )
    for i in range(n_y):
        for j in range(n_z):
            index[pl.ds((i * n_z + j) * own, own), :] = cols[
                pl.ds((i * n_dev + j * 2 + x) * own, own), :
            ]
    close_round(0)
    open_round(1)
    picks = groups * own
    wanted = index[...]
    for k in range(rows // LANES):
        lane = lax.broadcasted_iota(jnp.int32, (picks, LANES), 1) + k * LANES
        base[:, k * LANES:(k + 1) * LANES] = sign_of(wanted & lane, row_bits).astype(jnp.bfloat16)

    owner_signs = [
        sign_of(wanted & ((grp * n_dev + dev) * rows), all_bits)
        for grp, dev in ((me_g, me_d), (pair_g, me_d), (me_g, twin_d), (pair_g, twin_d))
    ]

    def term(h, slot, flip_bits, grp, dev):
        signs = base[...]
        toggles = (1 - 2 * flip_bits).astype(f32).astype(jnp.bfloat16)
        signs = jnp.concatenate(
            [
                signs[:, k * LANES:(k + 1) * LANES] * toggles[k:k + 1, :]
                for k in range(rows // LANES)
            ],
            axis=1,
        )
        packed = slabs[h, slot]
        high, mid, low = split3(packed)
        high_s, mid_s, low_s = split3(swap(packed))
        right = jnp.concatenate(
            [
                jnp.concatenate([jnp.where(left, high, mid_s), low], axis=1),
                jnp.concatenate([jnp.where(left, high_s, mid), low_s], axis=1),
            ],
            axis=0,
        )
        product = jnp.dot(signs, right, preferred_element_type=f32)
        first, last = product[:, :width], product[:, width:]
        return (first + swap(first) + last) * owner_signs[slot]

    def give(h, i, j):
        to_y, to_z = lax.rem(y + i, n_y), lax.rem(z + j, n_z)
        remote(
            part.at[h, to_y * n_z + to_z], blocks.at[h, mine], rs_send.at[h], rs_recv.at[h],
            to_y * 2 + core, to_z * 2 + x,
        ).start()

    for k in range(1, len(rounds) - 1):
        close_round(k)
        open_round(k + 1)
    totals = [term(h, 0, flip_ref[...], me_g, me_d) for h in range(2)]
    close_round(len(rounds) - 1)
    open_round(len(rounds))
    flip_copies[0].wait_recv()
    for h in range(2):
        pair[h].wait_recv()
        totals[h] = totals[h] + term(h, 1, flips[0], pair_g, me_d)
    flip_copies[1].wait_recv()
    flip_copies[2].start()
    forward = []
    for h in range(2):
        for c in range(pieces // 2):
            at = pl.ds(c * piece, piece)
            k = h * (pieces // 2) + c
            twin[k].wait_recv()
            copy = remote(
                slabs.at[h, 2, at], slabs.at[h, 3, at],
                fwd_send.at[k], fwd_recv.at[k], pair_g, me_d,
            )
            copy.start()
            forward.append(copy)
        total = totals[h] + term(h, 2, flips[1], me_g, twin_d)
        if h == 0:
            flip_copies[2].wait_recv()
        for copy in forward[h * (pieces // 2):]:
            copy.wait_recv()
        total = total + term(h, 3, flips[2], pair_g, twin_d)
        total = total.reshape(groups, own, width)
        part[h] = jnp.where(
            left.reshape(1, 1, width), total[:, :own // 2], swap(total[:, own // 2:])
        )
        if h == 0:
            close_round(len(rounds))
            open_round(len(rounds) + 1)
        for i in range(n_y - 1, -1, -1):
            loop(n_z - (i == 0), lambda j: give(h, i, j + (i == 0)))
        blocks[h, mine] = part[h, mine]
    sums = []
    for h in range(2):
        others = blocks.at[h, pl.ds(0, groups - 1)]
        pltpu.make_async_copy(others, others, rs_recv.at[h]).wait()
        summed = blocks[h, 0]
        for i in range(1, groups):
            summed = summed + blocks[h, i]
        sums.append(summed)
    sketch = jnp.concatenate(
        [
            jnp.where(left, sums[0], swap(sums[1])),
            jnp.where(left, swap(sums[0]), sums[1]),
        ],
        axis=0,
    )
    sketch = sketch * (1.0 / math.sqrt(rows * devices))
    sketch_ref[...] = sketch

    close_round(len(rounds) + 1)
    chunks = gfull.shape[0]
    across = min(chunks, n_dev // 2)
    first = (n_dev - across) // 2
    chunk = width // chunks
    linear = me_g * n_dev + me_d
    reducer = (me_g < chunks // across) & (me_d >= first) & (me_d < first + across)
    my_chunk = me_g * across + me_d - first
    gram = lax.dot_general(
        sketch, sketch, (((0,), (0,)), ((), ())),
        precision=lax.Precision.HIGHEST, preferred_element_type=f32,
    )
    gpart[...] = gram.reshape(chunks, chunk, width)
    turn = lax.rem(linear, chunks)
    for k in range(chunks):
        to = lax.rem(k + turn, chunks)
        to_g, to_d = lax.div(to, across), first + lax.rem(to, across)

        @pl.when((me_g != to_g) | (me_d != to_d))
        def _():
            remote(gpart.at[to], gslots.at[linear], g_send, g_recv, to_g, to_d).start()

    @pl.when(reducer)
    def _():
        gslots[linear] = gpart[my_chunk]
        rest = gslots.at[pl.ds(0, devices - 1)]
        pltpu.make_async_copy(rest, rest, g_recv).wait()
        result = jnp.sum(gslots[...], axis=0) * (1.0 / samples)
        reduced[...] = result
        gfull[my_chunk] = result

        def tell(i, j):
            remote(
                reduced, gfull.at[my_chunk], b_send, b_recv,
                lax.rem(me_g + i, n_grp), lax.rem(me_d + j, n_dev),
            ).start()

        for i in range(n_grp - 1, -1, -1):
            loop(n_dev - (i == 0), lambda j: tell(i, j + (i == 0)))
        most = gfull.at[pl.ds(0, chunks - 1)]
        pltpu.make_async_copy(most, most, b_recv).wait()
        pltpu.make_async_copy(rest, rest, b_send).wait()
        pltpu.make_async_copy(most, most, g_send).wait()

    @pl.when(jnp.logical_not(reducer))
    def _():
        pltpu.make_async_copy(gfull, gfull, b_recv).wait()
        pltpu.make_async_copy(gfull, gfull, g_send).wait()

    gram_ref[...] = gfull[...].reshape(width, width)
    for copy in twin + forward + flip_copies + pair:
        copy.wait_send()
    for h in range(2):
        others = blocks.at[h, pl.ds(0, groups - 1)]
        pltpu.make_async_copy(others, others, rs_send.at[h]).wait()


def split2(value):
    high = value.astype(jnp.bfloat16)
    return high, (value - high.astype(jnp.float32)).astype(jnp.bfloat16)


def plane_kernel(
    n_grp, n_dev, rows, own,
    x_hbm, flip_hbm, sample_hbm, sketch_ref, gram_ref,
    x_ref, flip_ref, sample_ref, turned, slabs, signs, peer_signs, lent, borrowed, part, blocks, mixed, cols,
    turn_back, gram_out, gram_in, gram_sum, gram_far,
    load_sem, in_send, in_recv, c_send, c_recv, z_send, z_recv, out_send, out_recv,
    g_send, g_recv, h_send, h_recv, ready,
):
    f32, bf16 = jnp.float32, jnp.bfloat16
    width = x_ref.shape[1]
    n_y, n_z = n_grp // 2, n_dev // 2
    chips = n_y * 2
    chunks, mine = slabs.shape[0], slabs.shape[2]
    band = chips * mine
    span = n_dev * own // LANES
    samples = sample_ref.shape[0] * LANES
    picks = n_y * LANES
    row_bits = rows.bit_length() - 1
    all_bits = (rows * n_grp * n_dev).bit_length() - 1
    me_g, me_d = lax.axis_index("grp"), lax.axis_index("dev")
    core, y = lax.rem(me_g, 2), lax.div(me_g, 2)
    x, z = lax.rem(me_d, 2), lax.div(me_d, 2)
    me = y * 2 + x

    plane = [(a, k) for a in range(n_y - 1, -1, -1) for k in (1, 0) if a or k]
    far, first, final = [], 0, n_z - 1
    for _ in range(n_z - 1):
        down = z - first >= final - z
        far.append(jnp.where(down, first, final))
        first, final = first + jnp.where(down, 1, 0), final - jnp.where(down, 0, 1)
    others = [lax.rem(z + d, n_z) for d in range(1, n_z)]
    sibling = (me_g + 1 - 2 * core, me_d)

    def across(a, k):
        to_y, to_x = lax.rem(y + a, n_y), lax.rem(x + k, 2)
        return (to_y * 2 + core, z * 2 + to_x), to_y * 2 + to_x

    def along(to_z):
        return me_g, to_z * 2 + x

    def arrival(slot, sem):
        pltpu.make_async_copy(slot, slot, sem).wait()

    def remote(src, dst, send, recv, at):
        return pltpu.make_async_remote_copy(
            src_ref=src, dst_ref=dst, send_sem=send, recv_sem=recv,
            device_id=at, device_id_type=MESH,
        )


    barrier = pltpu.get_barrier_semaphore()
    loads = [
        pltpu.make_async_copy(x_hbm, x_ref, load_sem.at[0]),
        pltpu.make_async_copy(flip_hbm, flip_ref, load_sem.at[1]),
        pltpu.make_async_copy(sample_hbm, sample_ref, load_sem.at[2]),
    ]
    for copy in loads:
        copy.start()
    greeted = [across(*at)[0] for at in plane] + [sibling]
    for at in greeted:
        pl.semaphore_signal(barrier, inc=1, device_id=at, device_id_type=MESH)
    for step in range(1, n_z):
        @pl.when(z + step < n_z)
        def _():
            pl.semaphore_signal(barrier, inc=1, device_id=along(z + step), device_id_type=MESH)
    for copy in loads:
        copy.wait()

    toggles = (1 - 2 * flip_ref[...]).astype(f32)
    for k in range(rows // LANES):
        at = slice(k * LANES, (k + 1) * LANES)
        turned[:, at] = jnp.transpose(x_ref[at, :]) * toggles[k:k + 1, :]
    pl.semaphore_wait(barrier, len(greeted) + z)

    sent, swaps, passed, given, around, last = [], [], [], [], [], []
    low = lax.broadcasted_iota(jnp.int32, (16, LANES), 0)
    for k in range(2):
        for m, at in enumerate(plane):
            to, chip = across(*at)
            copy = remote(
                turned.at[pl.ds(pl.multiple_of(k * band + chip * mine, mine), mine)],
                slabs.at[k, me], in_send.at[k, m], in_recv.at[k, m], to,
            )
            copy.start()
            sent.append(copy)
        slabs[k, me] = turned[pl.ds(pl.multiple_of(k * band + me * mine, mine), mine), :]
        if k == 0:
            for step in range(1, n_z):
                @pl.when(z >= step)
                def _():
                    pl.semaphore_signal(ready, inc=1, device_id=along(z - step), device_id_type=MESH)
        owner = core if k else 1 - core
        for i, to_z in enumerate(far + [z]):
            for j in range(n_y):
                at = slice(i * picks + j * LANES, i * picks + (j + 1) * LANES)
                wanted = sample_ref[pl.ds((j * 2 + owner) * span + to_z, 1), :]
                wide = jnp.broadcast_to(wanted, (16, LANES))
                pieces = [sign_of(wide & low, 16).astype(bf16)]
                for bit in range(4, row_bits):
                    factor = (1 - 2 * ((wide >> bit) & 1)).astype(f32).astype(bf16)
                    pieces += [piece * factor for piece in pieces]
                for r, piece in enumerate(pieces):
                    signs[k, r * 16:(r + 1) * 16, at] = piece
                wide = wide[:8]
                for q in range(chips):
                    holder = ((q // 2 * 2 + core) * n_dev + z * 2 + q % 2) * rows
                    peer_signs[k, q, :, at] = sign_of(wide & holder, all_bits)

    def halves(k):
        high, mid = split2(slabs[k].reshape(band, rows))
        return jnp.concatenate([high, mid], axis=0)

    def partial(left, r):
        product = jnp.dot(left, signs[r], preferred_element_type=f32)
        product = product[:band] + product[band:]
        total = None
        for q in range(chips):
            term = product[q * mine:(q + 1) * mine].reshape(mine // 8, 8, n_z * picks) * peer_signs[r, q][None]
            total = term if total is None else total + term
        return total.reshape(mine, n_z * picks)

    def settle(k):
        swaps[k].wait_recv()
        for i, to_z in enumerate(far + [z]):
            at = slice(i * picks, (i + 1) * picks)
            part[k, i] = part[k, i] + borrowed[k, :, at]
            if i < n_z - 1:
                copy = remote(
                    part.at[k, i], blocks.at[k, z], z_send.at[k, i], z_recv.at[k, z], along(to_z)
                )
                copy.start()
                passed.append(copy)

    for k in range(chunks):
        for copy in sent[k * len(plane):(k + 1) * len(plane)]:
            copy.wait_recv()
        left = halves(k)
        lent[k] = partial(left, 0)
        copy = remote(lent.at[k], borrowed.at[k], c_send.at[k], c_recv.at[k], sibling)
        copy.start()
        swaps.append(copy)
        if k == 0:
            @pl.when(z < n_z - 1)
            def _():
                pl.semaphore_wait(ready, n_z - 1 - z)
        else:
            settle(k - 1)
        mixture = partial(left, 1)
        for i in range(n_z):
            part[k, i] = mixture[:, i * picks:(i + 1) * picks]
    settle(chunks - 1)
    for k in range(chunks):
        total = part[k, n_z - 1]
        for from_z in others:
            arrival(blocks.at[k, from_z], z_recv.at[k, from_z])
            total = total + blocks[k, from_z]
        mixed[k] = total * (1.0 / math.sqrt(rows * n_grp * n_dev))
        for m, at in enumerate(plane):
            copy = remote(
                mixed.at[k], cols.at[k, me], out_send.at[k, m], out_recv.at[k, m], across(*at)[0]
            )
            copy.start()
            given.append(copy)
        cols[k, me] = mixed[k]

    right = None
    areas = [slice(0, band // 2), slice(band // 2, band // 2 + band)]
    for k in range(chunks):
        for copy in given[k * len(plane):(k + 1) * len(plane)]:
            copy.wait_recv()
        high, mid = split2(cols[k].reshape(band, picks))
        fresh = jnp.concatenate([high, high, mid], axis=1)
        right = fresh if right is None else jnp.concatenate([right, fresh], axis=0)
        gram = lax.dot_general(
            jnp.concatenate([high, mid, high], axis=1), right,
            (((1,), (1,)), ((), ())), preferred_element_type=f32,
        ) * (1.0 / samples)
        if k == 0:
            gram = jnp.concatenate([gram[:band // 2], gram[band // 2:]], axis=1)
        gram_out[areas[k]] = gram
        for i, to_z in enumerate(far):
            copy = remote(
                gram_out.at[areas[k]], gram_in.at[z, areas[k]], g_send.at[k, i], g_recv.at[k, z], along(to_z)
            )
            copy.start()
            around.append(copy)

    block = cols[:, :, :, pl.ds(pl.multiple_of(y * LANES, LANES), LANES)].reshape(width, LANES)
    turn_back[...] = jnp.transpose(block)
    sketch_ref[...] = turn_back[pl.ds(pl.multiple_of(x * own, own), own), :]
    for k in range(chunks):
        total = gram_out[areas[k]]
        for from_z in others:
            arrival(gram_in.at[from_z, areas[k]], g_recv.at[k, from_z])
            total = total + gram_in[from_z, areas[k]]
        gram_sum[areas[k]] = total
        copy = remote(gram_sum.at[areas[k]], gram_far.at[areas[k]], h_send.at[k], h_recv.at[k], sibling)
        copy.start()
        last.append(copy)
    for copy in last:
        copy.wait_recv()
    early, late = (gram_sum[at] + gram_far[at] for at in areas)
    early = jnp.concatenate([early[:, :band], early[:, band:]], axis=0)
    cross = jnp.transpose(late)[:band]
    gram_ref[:band, :] = jnp.concatenate([early, cross], axis=1)
    gram_ref[band:, :] = late
    for copy in sent + swaps + passed + given + around + last:
        copy.wait_send()


def general(matrix, flip_bits, sample_rows):
    rows, width = matrix.shape
    n_grp, n_dev = lax.axis_size("grp"), lax.axis_size("dev")
    devices = n_grp * n_dev
    samples = sample_rows.shape[0]
    own = samples // devices
    groups = devices // 4
    chunks = min(width // 8, devices // 2)
    chunk = width // chunks
    pieces = 4
    f32, i32 = jnp.float32, jnp.int32
    dma = pltpu.SemaphoreType.DMA
    vmem = pl.BlockSpec(memory_space=pltpu.VMEM)
    return pl.pallas_call(
        functools.partial(kernel, n_grp, n_dev, rows, own),
        out_shape=(
            pltpu.VMEM((own, width), f32),
            pltpu.VMEM((width, width), f32),
        ),
        in_specs=[pl.BlockSpec(memory_space=pl.ANY)] * 3,
        out_specs=(vmem, vmem),
        scratch_shapes=[
            pltpu.VMEM((rows // LANES, LANES), i32),
            pltpu.VMEM((samples // LANES, LANES), i32),
            pltpu.VMEM((rows, width), f32),
            pltpu.VMEM((2, 4, rows // 2, width), f32),
            pltpu.VMEM((3, rows // LANES, LANES), i32),
            pltpu.VMEM((samples // 2, LANES), i32),
            pltpu.VMEM((groups * own, LANES), i32),
            pltpu.VMEM((groups * own, rows), jnp.bfloat16),
            pltpu.VMEM((2, groups, own // 2, width), f32),
            pltpu.VMEM((2, groups, own // 2, width), f32),
            pltpu.VMEM((chunks, chunk, width), f32),
            pltpu.VMEM((devices, chunk, width), f32),
            pltpu.VMEM((chunks, chunk, width), f32),
            pltpu.VMEM((chunk, width), f32),
            dma((3,)), dma((2,)), dma((2,)), dma((pieces,)), dma((pieces,)), dma((pieces,)), dma((pieces,)),
            dma((3,)), dma((3,)), dma((2,)), dma((2,)), dma, dma, dma, dma,
            pltpu.SemaphoreType.REGULAR((16,)),
        ],
        compiler_params=pltpu.CompilerParams(collective_id=0, has_side_effects=True),
    )(
        matrix,
        flip_bits.reshape(rows // LANES, LANES),
        sample_rows.reshape(samples // LANES, LANES),
    )


def plane_body(matrix, flip_bits, sample_rows):
    rows, width = matrix.shape
    n_grp, n_dev = lax.axis_size("grp"), lax.axis_size("dev")
    samples = sample_rows.shape[0]
    own = samples // (n_grp * n_dev)
    n_y, n_z, chips = n_grp // 2, n_dev // 2, n_grp
    chunks = 2
    mine, band, picks = width // (chips * chunks), width // chunks, n_y * LANES
    f32, i32, bf16 = jnp.float32, jnp.int32, jnp.bfloat16
    dma = pltpu.SemaphoreType.DMA
    vmem = pl.BlockSpec(memory_space=pltpu.VMEM)
    return pl.pallas_call(
        functools.partial(plane_kernel, n_grp, n_dev, rows, own),
        out_shape=(pltpu.VMEM((own, width), f32), pltpu.VMEM((width, width), f32)),
        in_specs=[pl.BlockSpec(memory_space=pl.ANY)] * 3,
        out_specs=(vmem, vmem),
        scratch_shapes=[
            pltpu.VMEM((rows, width), f32),
            pltpu.VMEM((rows // LANES, LANES), i32),
            pltpu.VMEM((samples // LANES, LANES), i32),
            pltpu.VMEM((width, rows), f32),
            pltpu.VMEM((chunks, chips, mine, rows), f32),
            pltpu.VMEM((2, rows, n_z * picks), bf16),
            pltpu.VMEM((2, chips, 8, n_z * picks), f32),
            pltpu.VMEM((chunks, mine, n_z * picks), f32),
            pltpu.VMEM((chunks, mine, n_z * picks), f32),
            pltpu.VMEM((chunks, n_z, mine, picks), f32),
            pltpu.VMEM((chunks, n_z, mine, picks), f32),
            pltpu.VMEM((chunks, mine, picks), f32),
            pltpu.VMEM((chunks, chips, mine, picks), f32),
            pltpu.VMEM((LANES, width), f32),
            pltpu.VMEM((band // 2 + band, width), f32),
            pltpu.VMEM((n_z, band // 2 + band, width), f32),
            pltpu.VMEM((band // 2 + band, width), f32),
            pltpu.VMEM((band // 2 + band, width), f32),
            dma((3,)), dma((chunks, chips - 1)), dma((chunks, chips - 1)), dma((chunks,)), dma((chunks,)),
            dma((chunks, n_z - 1)), dma((chunks, n_z)), dma((chunks, chips - 1)), dma((chunks, chips - 1)),
            dma((chunks, n_z - 1)), dma((chunks, n_z)), dma((chunks,)), dma((chunks,)),
            pltpu.SemaphoreType.REGULAR,
        ],
        compiler_params=pltpu.CompilerParams(collective_id=0, has_side_effects=True),
    )(
        matrix,
        flip_bits.reshape(rows // LANES, LANES),
        sample_rows.reshape(samples // LANES, LANES),
    )


def body(matrix, flip_bits, sample_rows):
    rows, width = matrix.shape
    n_grp, n_dev = lax.axis_size("grp"), lax.axis_size("dev")
    paired = sample_rows.shape[0] * 2 == n_grp * n_dev * LANES
    tiled = width == LANES and width % (n_grp * 16) == 0
    if paired and tiled and rows % LANES == 0:
        return plane_body(matrix, flip_bits, sample_rows)
    return general(matrix, flip_bits, sample_rows)


def solution(mesh):
    return jax.shard_map(
        body,
        mesh=mesh,
        in_specs=(P(("grp", "dev"), None), P(("grp", "dev")), P()),
        out_specs=(P(("grp", "dev"), None), P()),
        check_vma=False,
    )
```

```python
import functools
import math

import jax
import jax.numpy as jnp
from jax import lax
from jax.experimental import pallas as pl
from jax.experimental.pallas import tpu as pltpu
from jax.sharding import PartitionSpec as P

MESH = pl.DeviceIdType.MESH
LANES = 128


def loop(count, fn):
    if count <= 8:
        for step in range(count):
            fn(step)
    else:
        lax.fori_loop(0, count, lambda step, carry: (fn(step), carry)[1], 0)


def parity(bits, width):
    shift = 1
    while shift * 2 < width:
        shift *= 2
    while shift:
        bits = bits ^ (bits >> shift)
        shift //= 2
    return bits & 1


def sign_of(bits, width):
    return (1 - 2 * parity(bits, width)).astype(jnp.float32)


def split3(value):
    high = value.astype(jnp.bfloat16)
    rest = value - high.astype(jnp.float32)
    mid = rest.astype(jnp.bfloat16)
    low = (rest - mid.astype(jnp.float32)).astype(jnp.bfloat16)
    return high, mid, low


def kernel(
    n_grp, n_dev, rows, own,
    x_ref, flip_hbm, sample_hbm, sketch_ref, gram_ref,
    flip_ref, sample_ref, x_full, slabs, flips, cols, index, base, part, blocks, gpart, gslots, gfull, reduced,
    load_sem, pair_send, pair_recv, twin_send, twin_recv, fwd_send, fwd_recv,
    flip_send, flip_recv, rs_send, rs_recv, g_send, g_recv, b_send, b_recv,
    ready,
):
    f32 = jnp.float32
    devices = n_grp * n_dev
    n_y, n_z = n_grp // 2, n_dev // 2
    groups = n_y * n_z
    width = x_ref.shape[1]
    pieces = twin_send.shape[0]
    piece = rows // pieces
    samples = sample_hbm.shape[0] * LANES
    row_bits = rows.bit_length() - 1
    all_bits = (rows * devices).bit_length() - 1
    me_g, me_d = lax.axis_index("grp"), lax.axis_index("dev")
    core, y = lax.rem(me_g, 2), lax.div(me_g, 2)
    x, z = lax.rem(me_d, 2), lax.div(me_d, 2)
    pair_g = me_g + 1 - 2 * core
    twin_d = me_d + 1 - 2 * x
    mine = y * n_z + z

    def remote(src, dst, send, recv, grp, dev):
        return pltpu.make_async_remote_copy(
            src_ref=src, dst_ref=dst, send_sem=send, recv_sem=recv,
            device_id=(grp, dev), device_id_type=MESH,
        )

    barrier = pltpu.get_barrier_semaphore()

    def signal(sem, grp, dev):
        pl.semaphore_signal(sem, inc=1, device_id=(grp, dev), device_id_type=MESH)

    def along_y(step):
        return me_g + 2 * step, me_d

    def along_z(step):
        return me_g, me_d + 2 * step

    def tell_line(sem, at, size, reach, along):
        for step in range(1, min(reach, size - 1) + 1):
            @pl.when(at >= step)
            def _():
                signal(sem, *along(-step))

            @pl.when(at + step < size)
            def _():
                signal(sem, *along(step))

    def line_count(at, size, reach):
        return jnp.minimum(at, reach) + jnp.minimum(size - 1 - at, reach)

    signal(barrier, pair_g, me_d)
    signal(barrier, me_g, twin_d)
    tell_line(barrier, y, n_y, 1, along_y)
    tell_line(barrier, z, n_z, 1, along_z)

    loads = [
        pltpu.make_async_copy(sample_hbm, sample_ref, load_sem.at[0]),
        pltpu.make_async_copy(flip_hbm, flip_ref, load_sem.at[1]),
        pltpu.make_async_copy(x_ref, x_full, load_sem.at[2]),
    ]
    for copy in loads:
        copy.start()
    pl.semaphore_wait(barrier, 2 + line_count(y, n_y, 1) + line_count(z, n_z, 1))

    rounds = []
    for at, size, along in ((z, n_z, along_z), (y, n_y, along_y)):
        reach = 1
        while reach < size - 1:
            rounds.append((at, size, reach, along))
            reach *= 2
    rounds.append((y, n_y, n_y - 1, along_y))

    def open_round(k):
        if k < len(rounds):
            at, size, reach, along = rounds[k]
            tell_line(ready.at[k], at, size, reach, along)
        elif k == len(rounds):
            signal(ready.at[k], me_g, twin_d)
        else:
            signal(ready.at[k], pair_g, me_d)

    def close_round(k):
        if k < len(rounds):
            at, size, reach, along = rounds[k]
            pl.semaphore_wait(ready.at[k], line_count(at, size, reach))
        else:
            pl.semaphore_wait(ready.at[k], 1)

    half = width // 2
    left = lax.broadcasted_iota(jnp.int32, (1, width), 1) < half

    def swap(value):
        return pltpu.roll(value, half, value.ndim - 1)

    for copy in loads:
        copy.wait()
    top, bottom = x_full[pl.ds(0, rows // 2), :], x_full[pl.ds(rows // 2, rows // 2), :]
    slabs[0, 0] = jnp.where(left, top, swap(bottom))
    slabs[1, 0] = jnp.where(left, swap(top), bottom)
    twin, pair = [], []
    for h in range(2):
        for c in range(pieces // 2):
            at = pl.ds(c * piece, piece)
            k = h * (pieces // 2) + c
            copy = remote(
                slabs.at[h, 0, at], slabs.at[h, 2, at],
                twin_send.at[k], twin_recv.at[k], me_g, twin_d,
            )
            copy.start()
            twin.append(copy)
    for h in range(2):
        copy = remote(
            slabs.at[h, 0], slabs.at[h, 1], pair_send.at[h], pair_recv.at[h], pair_g, me_d
        )
        copy.start()
        pair.append(copy)
    flip_copies = [
        remote(flip_ref, flips.at[0], flip_send.at[0], flip_recv.at[0], pair_g, me_d),
        remote(flip_ref, flips.at[1], flip_send.at[1], flip_recv.at[1], me_g, twin_d),
        remote(flips.at[1], flips.at[2], flip_send.at[2], flip_recv.at[2], pair_g, me_d),
    ]
    open_round(0)
    for copy in flip_copies[:2]:
        copy.start()

    span = n_dev * own // LANES
    for i in range(n_y):
        for r in range(span):
            line = sample_ref[pl.ds((i * 2 + core) * span + r, 1), :]
            cols[pl.ds((i * span + r) * LANES, LANES), :] = jnp.transpose(
                jnp.broadcast_to(line, (LANES, LANES))
            )
    for i in range(n_y):
        for j in range(n_z):
            index[pl.ds((i * n_z + j) * own, own), :] = cols[
                pl.ds((i * n_dev + j * 2 + x) * own, own), :
            ]
    close_round(0)
    open_round(1)
    picks = groups * own
    wanted = index[...]
    for k in range(rows // LANES):
        lane = lax.broadcasted_iota(jnp.int32, (picks, LANES), 1) + k * LANES
        base[:, k * LANES:(k + 1) * LANES] = sign_of(wanted & lane, row_bits).astype(jnp.bfloat16)

    owner_signs = [
        sign_of(wanted & ((grp * n_dev + dev) * rows), all_bits)
        for grp, dev in ((me_g, me_d), (pair_g, me_d), (me_g, twin_d), (pair_g, twin_d))
    ]

    def term(h, slot, flip_bits, grp, dev):
        signs = base[...]
        toggles = (1 - 2 * flip_bits).astype(f32).astype(jnp.bfloat16)
        signs = jnp.concatenate(
            [
                signs[:, k * LANES:(k + 1) * LANES] * toggles[k:k + 1, :]
                for k in range(rows // LANES)
            ],
            axis=1,
        )
        packed = slabs[h, slot]
        high, mid, low = split3(packed)
        high_s, mid_s, low_s = split3(swap(packed))
        right = jnp.concatenate(
            [
                jnp.concatenate([jnp.where(left, high, mid_s), low], axis=1),
                jnp.concatenate([jnp.where(left, high_s, mid), low_s], axis=1),
            ],
            axis=0,
        )
        product = jnp.dot(signs, right, preferred_element_type=f32)
        first, last = product[:, :width], product[:, width:]
        return (first + swap(first) + last) * owner_signs[slot]

    def give(h, i, j):
        to_y, to_z = lax.rem(y + i, n_y), lax.rem(z + j, n_z)
        remote(
            part.at[h, to_y * n_z + to_z], blocks.at[h, mine], rs_send.at[h], rs_recv.at[h],
            to_y * 2 + core, to_z * 2 + x,
        ).start()

    for k in range(1, len(rounds) - 1):
        close_round(k)
        open_round(k + 1)
    totals = [term(h, 0, flip_ref[...], me_g, me_d) for h in range(2)]
    close_round(len(rounds) - 1)
    open_round(len(rounds))
    flip_copies[0].wait_recv()
    for h in range(2):
        pair[h].wait_recv()
        totals[h] = totals[h] + term(h, 1, flips[0], pair_g, me_d)
    flip_copies[1].wait_recv()
    flip_copies[2].start()
    forward = []
    for h in range(2):
        for c in range(pieces // 2):
            at = pl.ds(c * piece, piece)
            k = h * (pieces // 2) + c
            twin[k].wait_recv()
            copy = remote(
                slabs.at[h, 2, at], slabs.at[h, 3, at],
                fwd_send.at[k], fwd_recv.at[k], pair_g, me_d,
            )
            copy.start()
            forward.append(copy)
        total = totals[h] + term(h, 2, flips[1], me_g, twin_d)
        if h == 0:
            flip_copies[2].wait_recv()
        for copy in forward[h * (pieces // 2):]:
            copy.wait_recv()
        total = total + term(h, 3, flips[2], pair_g, twin_d)
        total = total.reshape(groups, own, width)
        part[h] = jnp.where(
            left.reshape(1, 1, width), total[:, :own // 2], swap(total[:, own // 2:])
        )
        if h == 0:
            close_round(len(rounds))
            open_round(len(rounds) + 1)
        for i in range(n_y - 1, -1, -1):
            loop(n_z - (i == 0), lambda j: give(h, i, j + (i == 0)))
        blocks[h, mine] = part[h, mine]
    sums = []
    for h in range(2):
        others = blocks.at[h, pl.ds(0, groups - 1)]
        pltpu.make_async_copy(others, others, rs_recv.at[h]).wait()
        summed = blocks[h, 0]
        for i in range(1, groups):
            summed = summed + blocks[h, i]
        sums.append(summed)
    sketch = jnp.concatenate(
        [
            jnp.where(left, sums[0], swap(sums[1])),
            jnp.where(left, swap(sums[0]), sums[1]),
        ],
        axis=0,
    )
    sketch = sketch * (1.0 / math.sqrt(rows * devices))
    sketch_ref[...] = sketch

    close_round(len(rounds) + 1)
    chunks = gfull.shape[0]
    across = min(chunks, n_dev // 2)
    first = (n_dev - across) // 2
    chunk = width // chunks
    linear = me_g * n_dev + me_d
    reducer = (me_g < chunks // across) & (me_d >= first) & (me_d < first + across)
    my_chunk = me_g * across + me_d - first
    gram = lax.dot_general(
        sketch, sketch, (((0,), (0,)), ((), ())),
        precision=lax.Precision.HIGHEST, preferred_element_type=f32,
    )
    gpart[...] = gram.reshape(chunks, chunk, width)
    turn = lax.rem(linear, chunks)
    for k in range(chunks):
        to = lax.rem(k + turn, chunks)
        to_g, to_d = lax.div(to, across), first + lax.rem(to, across)

        @pl.when((me_g != to_g) | (me_d != to_d))
        def _():
            remote(gpart.at[to], gslots.at[linear], g_send, g_recv, to_g, to_d).start()

    @pl.when(reducer)
    def _():
        gslots[linear] = gpart[my_chunk]
        rest = gslots.at[pl.ds(0, devices - 1)]
        pltpu.make_async_copy(rest, rest, g_recv).wait()
        result = jnp.sum(gslots[...], axis=0) * (1.0 / samples)
        reduced[...] = result
        gfull[my_chunk] = result

        def tell(i, j):
            remote(
                reduced, gfull.at[my_chunk], b_send, b_recv,
                lax.rem(me_g + i, n_grp), lax.rem(me_d + j, n_dev),
            ).start()

        for i in range(n_grp - 1, -1, -1):
            loop(n_dev - (i == 0), lambda j: tell(i, j + (i == 0)))
        most = gfull.at[pl.ds(0, chunks - 1)]
        pltpu.make_async_copy(most, most, b_recv).wait()
        pltpu.make_async_copy(rest, rest, b_send).wait()
        pltpu.make_async_copy(most, most, g_send).wait()

    @pl.when(jnp.logical_not(reducer))
    def _():
        pltpu.make_async_copy(gfull, gfull, b_recv).wait()
        pltpu.make_async_copy(gfull, gfull, g_send).wait()

    gram_ref[...] = gfull[...].reshape(width, width)
    for copy in twin + forward + flip_copies + pair:
        copy.wait_send()
    for h in range(2):
        others = blocks.at[h, pl.ds(0, groups - 1)]
        pltpu.make_async_copy(others, others, rs_send.at[h]).wait()


def split2(value):
    high = value.astype(jnp.bfloat16)
    return high, (value - high.astype(jnp.float32)).astype(jnp.bfloat16)


def plane_kernel(
    n_grp, n_dev, rows, own,
    x_hbm, flip_hbm, sample_hbm, sketch_ref, gram_ref,
    x_ref, flip_ref, sample_ref, turned, slabs, signs, peer_signs, lent, borrowed, part, blocks, mixed, cols,
    turn_back, gram_part, gram_sib, gram_out, gram_in, gram_full,
    load_sem, in_send, in_recv, c_send, c_recv, z_send, z_recv, out_send, out_recv,
    s_send, s_recv, g_send, g_recv, h_send, h_recv, ready,
):
    f32, bf16 = jnp.float32, jnp.bfloat16
    width = x_ref.shape[1]
    n_y, n_z = n_grp // 2, n_dev // 2
    chips = n_y * 2
    chunks, mine = slabs.shape[0], slabs.shape[2]
    band = chips * mine
    span = n_dev * own // LANES
    samples = sample_ref.shape[0] * LANES
    picks = n_y * LANES
    row_bits = rows.bit_length() - 1
    all_bits = (rows * n_grp * n_dev).bit_length() - 1
    me_g, me_d = lax.axis_index("grp"), lax.axis_index("dev")
    core, y = lax.rem(me_g, 2), lax.div(me_g, 2)
    x, z = lax.rem(me_d, 2), lax.div(me_d, 2)
    me = y * 2 + x

    plane = [(a, k) for a in range(n_y - 1, -1, -1) for k in (1, 0) if a or k]
    far, first, final = [], 0, n_z - 1
    for _ in range(n_z - 1):
        down = z - first >= final - z
        far.append(jnp.where(down, first, final))
        first, final = first + jnp.where(down, 1, 0), final - jnp.where(down, 0, 1)
    others = [lax.rem(z + d, n_z) for d in range(1, n_z)]
    sibling = (me_g + 1 - 2 * core, me_d)

    def across(a, k):
        to_y, to_x = lax.rem(y + a, n_y), lax.rem(x + k, 2)
        return (to_y * 2 + core, z * 2 + to_x), to_y * 2 + to_x

    def along(to_z):
        return me_g, to_z * 2 + x

    def arrival(slot, sem):
        pltpu.make_async_copy(slot, slot, sem).wait()

    def remote(src, dst, send, recv, at):
        return pltpu.make_async_remote_copy(
            src_ref=src, dst_ref=dst, send_sem=send, recv_sem=recv,
            device_id=at, device_id_type=MESH,
        )


    barrier = pltpu.get_barrier_semaphore()
    loads = [
        pltpu.make_async_copy(x_hbm, x_ref, load_sem.at[0]),
        pltpu.make_async_copy(flip_hbm, flip_ref, load_sem.at[1]),
        pltpu.make_async_copy(sample_hbm, sample_ref, load_sem.at[2]),
    ]
    for copy in loads:
        copy.start()
    greeted = [across(*at)[0] for at in plane] + [sibling]
    for at in greeted:
        pl.semaphore_signal(barrier, inc=1, device_id=at, device_id_type=MESH)
    for step in range(1, n_z):
        @pl.when(z + step < n_z)
        def _():
            pl.semaphore_signal(barrier, inc=1, device_id=along(z + step), device_id_type=MESH)
    for copy in loads:
        copy.wait()

    toggles = (1 - 2 * flip_ref[...]).astype(f32)
    for k in range(rows // LANES):
        at = slice(k * LANES, (k + 1) * LANES)
        turned[:, at] = jnp.transpose(x_ref[at, :]) * toggles[k:k + 1, :]
    pl.semaphore_wait(barrier, len(greeted) + z)

    sent, swaps, passed, given, around, last = [], [], [], [], [], []
    low = lax.broadcasted_iota(jnp.int32, (16, LANES), 0)
    for k in range(2):
        for m, at in enumerate(plane):
            to, chip = across(*at)
            copy = remote(
                turned.at[pl.ds(pl.multiple_of(k * band + chip * mine, mine), mine)],
                slabs.at[k, me], in_send.at[k, m], in_recv.at[k, m], to,
            )
            copy.start()
            sent.append(copy)
        slabs[k, me] = turned[pl.ds(pl.multiple_of(k * band + me * mine, mine), mine), :]
        if k == 0:
            for step in range(1, n_z):
                @pl.when(z >= step)
                def _():
                    pl.semaphore_signal(ready, inc=1, device_id=along(z - step), device_id_type=MESH)
        owner = core if k else 1 - core
        for i, to_z in enumerate(far + [z]):
            for j in range(n_y):
                at = slice(i * picks + j * LANES, i * picks + (j + 1) * LANES)
                wanted = sample_ref[pl.ds((j * 2 + owner) * span + to_z, 1), :]
                wide = jnp.broadcast_to(wanted, (16, LANES))
                pieces = [sign_of(wide & low, 16).astype(bf16)]
                for bit in range(4, row_bits):
                    factor = (1 - 2 * ((wide >> bit) & 1)).astype(f32).astype(bf16)
                    pieces += [piece * factor for piece in pieces]
                for r, piece in enumerate(pieces):
                    signs[k, r * 16:(r + 1) * 16, at] = piece
                wide = wide[:8]
                for q in range(chips):
                    holder = ((q // 2 * 2 + core) * n_dev + z * 2 + q % 2) * rows
                    peer_signs[k, q, :, at] = sign_of(wide & holder, all_bits)

    def halves(k):
        high, mid = split2(slabs[k].reshape(band, rows))
        return jnp.concatenate([high, mid], axis=0)

    def partial(left, r):
        product = jnp.dot(left, signs[r], preferred_element_type=f32)
        product = product[:band] + product[band:]
        total = None
        for q in range(chips):
            term = product[q * mine:(q + 1) * mine].reshape(mine // 8, 8, n_z * picks) * peer_signs[r, q][None]
            total = term if total is None else total + term
        return total.reshape(mine, n_z * picks)

    def settle(k):
        swaps[k].wait_recv()
        for i, to_z in enumerate(far + [z]):
            at = slice(i * picks, (i + 1) * picks)
            part[k, i] = part[k, i] + borrowed[k, :, at]
            if i < n_z - 1:
                copy = remote(
                    part.at[k, i], blocks.at[k, z], z_send.at[k, i], z_recv.at[k, z], along(to_z)
                )
                copy.start()
                passed.append(copy)

    for k in range(chunks):
        for copy in sent[k * len(plane):(k + 1) * len(plane)]:
            copy.wait_recv()
        left = halves(k)
        lent[k] = partial(left, 0)
        copy = remote(lent.at[k], borrowed.at[k], c_send.at[k], c_recv.at[k], sibling)
        copy.start()
        swaps.append(copy)
        if k == 0:
            @pl.when(z < n_z - 1)
            def _():
                pl.semaphore_wait(ready, n_z - 1 - z)
        else:
            settle(k - 1)
        mixture = partial(left, 1)
        for i in range(n_z):
            part[k, i] = mixture[:, i * picks:(i + 1) * picks]
    settle(chunks - 1)
    for k in range(chunks):
        total = part[k, n_z - 1]
        for from_z in others:
            arrival(blocks.at[k, from_z], z_recv.at[k, from_z])
            total = total + blocks[k, from_z]
        mixed[k] = total * (1.0 / math.sqrt(rows * n_grp * n_dev))
        for m, at in enumerate(plane):
            copy = remote(
                mixed.at[k], cols.at[k, me], out_send.at[k, m], out_recv.at[k, m], across(*at)[0]
            )
            copy.start()
            given.append(copy)
        cols[k, me] = mixed[k]

    right = None
    areas = [slice(0, band // 4), slice(band // 4, band // 4 + band // 2)]

    def spread(k):
        halves_in[k].wait_recv()
        gram_out[areas[k]] = gram_part[core, areas[k]] + gram_sib[areas[k]]
        for i, to_z in enumerate(far):
            copy = remote(
                gram_out.at[areas[k]], gram_in.at[z, areas[k]], g_send.at[k, i], g_recv.at[k, z], along(to_z)
            )
            copy.start()
            around.append(copy)

    halves_in = []
    for k in range(chunks):
        for copy in given[k * len(plane):(k + 1) * len(plane)]:
            copy.wait_recv()
        if k:
            spread(k - 1)
        high, mid = split2(cols[k].reshape(band, picks))
        fresh = jnp.concatenate([high, high, mid], axis=1)
        right = fresh if right is None else jnp.concatenate([right, fresh], axis=0)
        gram = lax.dot_general(
            jnp.concatenate([high, mid, high], axis=1), right,
            (((1,), (1,)), ((), ())), preferred_element_type=f32,
        ) * (1.0 / samples)
        if k == 0:
            gram = gram.reshape(2, 2, band // 4, band)
            gram = jnp.concatenate([gram[:, 0], gram[:, 1]], axis=2)
        gram_part[:, areas[k]] = gram.reshape(2, -1, width)
        copy = remote(
            gram_part.at[1 - core, areas[k]], gram_sib.at[areas[k]], s_send.at[k], s_recv.at[k], sibling
        )
        copy.start()
        halves_in.append(copy)

    block = cols[:, :, :, pl.ds(pl.multiple_of(y * LANES, LANES), LANES)].reshape(width, LANES)
    turn_back[...] = jnp.transpose(block)
    sketch_ref[...] = turn_back[pl.ds(pl.multiple_of(x * own, own), own), :]
    spread(chunks - 1)
    for k in range(chunks):
        total = gram_out[areas[k]]
        for from_z in others:
            arrival(gram_in.at[from_z, areas[k]], g_recv.at[k, from_z])
            total = total + gram_in[from_z, areas[k]]
        gram_full[core, areas[k]] = total
        here = gram_full.at[core, areas[k]]
        copy = remote(here, here, h_send.at[k], h_recv.at[k], sibling)
        copy.start()
        last.append(copy)
    for copy in last:
        copy.wait_recv()
    early, late = (gram_full[:, at] for at in areas)
    early = jnp.stack([early[:, :, :band], early[:, :, band:]], axis=1).reshape(band, band)
    late = late.reshape(band, width)
    cross = jnp.transpose(late)[:band]
    gram_ref[:band, :] = jnp.concatenate([early, cross], axis=1)
    gram_ref[band:, :] = late
    for copy in sent + swaps + passed + given + halves_in + around + last:
        copy.wait_send()


def general(matrix, flip_bits, sample_rows):
    rows, width = matrix.shape
    n_grp, n_dev = lax.axis_size("grp"), lax.axis_size("dev")
    devices = n_grp * n_dev
    samples = sample_rows.shape[0]
    own = samples // devices
    groups = devices // 4
    chunks = min(width // 8, devices // 2)
    chunk = width // chunks
    pieces = 4
    f32, i32 = jnp.float32, jnp.int32
    dma = pltpu.SemaphoreType.DMA
    vmem = pl.BlockSpec(memory_space=pltpu.VMEM)
    return pl.pallas_call(
        functools.partial(kernel, n_grp, n_dev, rows, own),
        out_shape=(
            pltpu.VMEM((own, width), f32),
            pltpu.VMEM((width, width), f32),
        ),
        in_specs=[pl.BlockSpec(memory_space=pl.ANY)] * 3,
        out_specs=(vmem, vmem),
        scratch_shapes=[
            pltpu.VMEM((rows // LANES, LANES), i32),
            pltpu.VMEM((samples // LANES, LANES), i32),
            pltpu.VMEM((rows, width), f32),
            pltpu.VMEM((2, 4, rows // 2, width), f32),
            pltpu.VMEM((3, rows // LANES, LANES), i32),
            pltpu.VMEM((samples // 2, LANES), i32),
            pltpu.VMEM((groups * own, LANES), i32),
            pltpu.VMEM((groups * own, rows), jnp.bfloat16),
            pltpu.VMEM((2, groups, own // 2, width), f32),
            pltpu.VMEM((2, groups, own // 2, width), f32),
            pltpu.VMEM((chunks, chunk, width), f32),
            pltpu.VMEM((devices, chunk, width), f32),
            pltpu.VMEM((chunks, chunk, width), f32),
            pltpu.VMEM((chunk, width), f32),
            dma((3,)), dma((2,)), dma((2,)), dma((pieces,)), dma((pieces,)), dma((pieces,)), dma((pieces,)),
            dma((3,)), dma((3,)), dma((2,)), dma((2,)), dma, dma, dma, dma,
            pltpu.SemaphoreType.REGULAR((16,)),
        ],
        compiler_params=pltpu.CompilerParams(collective_id=0, has_side_effects=True),
    )(
        matrix,
        flip_bits.reshape(rows // LANES, LANES),
        sample_rows.reshape(samples // LANES, LANES),
    )


def write_out(sketch_in, gram_in, sketch_ref, gram_ref, sem):
    copies = [
        pltpu.make_async_copy(gram_in, gram_ref, sem.at[0]),
        pltpu.make_async_copy(sketch_in, sketch_ref, sem.at[1]),
    ]
    for copy in copies:
        copy.start()
    for copy in copies:
        copy.wait()


def plane_body(matrix, flip_bits, sample_rows):
    rows, width = matrix.shape
    n_grp, n_dev = lax.axis_size("grp"), lax.axis_size("dev")
    samples = sample_rows.shape[0]
    own = samples // (n_grp * n_dev)
    n_y, n_z, chips = n_grp // 2, n_dev // 2, n_grp
    chunks = 2
    mine, band, picks = width // (chips * chunks), width // chunks, n_y * LANES
    f32, i32, bf16 = jnp.float32, jnp.int32, jnp.bfloat16
    dma = pltpu.SemaphoreType.DMA
    vmem = pl.BlockSpec(memory_space=pltpu.VMEM)
    sketch, gram = pl.pallas_call(
        functools.partial(plane_kernel, n_grp, n_dev, rows, own),
        out_shape=(pltpu.VMEM((own, width), f32), pltpu.VMEM((width, width), f32)),
        in_specs=[pl.BlockSpec(memory_space=pl.ANY)] * 3,
        out_specs=(vmem, vmem),
        scratch_shapes=[
            pltpu.VMEM((rows, width), f32),
            pltpu.VMEM((rows // LANES, LANES), i32),
            pltpu.VMEM((samples // LANES, LANES), i32),
            pltpu.VMEM((width, rows), f32),
            pltpu.VMEM((chunks, chips, mine, rows), f32),
            pltpu.VMEM((2, rows, n_z * picks), bf16),
            pltpu.VMEM((2, chips, 8, n_z * picks), f32),
            pltpu.VMEM((chunks, mine, n_z * picks), f32),
            pltpu.VMEM((chunks, mine, n_z * picks), f32),
            pltpu.VMEM((chunks, n_z, mine, picks), f32),
            pltpu.VMEM((chunks, n_z, mine, picks), f32),
            pltpu.VMEM((chunks, mine, picks), f32),
            pltpu.VMEM((chunks, chips, mine, picks), f32),
            pltpu.VMEM((LANES, width), f32),
            pltpu.VMEM((2, band * 3 // 4, width), f32),
            pltpu.VMEM((band * 3 // 4, width), f32),
            pltpu.VMEM((band * 3 // 4, width), f32),
            pltpu.VMEM((n_z, band * 3 // 4, width), f32),
            pltpu.VMEM((2, band * 3 // 4, width), f32),
            dma((3,)), dma((chunks, chips - 1)), dma((chunks, chips - 1)), dma((chunks,)), dma((chunks,)),
            dma((chunks, n_z - 1)), dma((chunks, n_z)), dma((chunks, chips - 1)), dma((chunks, chips - 1)),
            dma((chunks,)), dma((chunks,)), dma((chunks, n_z - 1)), dma((chunks, n_z)), dma((chunks,)), dma((chunks,)),
            pltpu.SemaphoreType.REGULAR,
        ],
        compiler_params=pltpu.CompilerParams(collective_id=0, has_side_effects=True),
    )(
        matrix,
        flip_bits.reshape(rows // LANES, LANES),
        sample_rows.reshape(samples // LANES, LANES),
    )
    hbm = pl.BlockSpec(memory_space=pl.ANY)
    return pl.pallas_call(
        write_out,
        out_shape=(jax.ShapeDtypeStruct((own, width), f32), jax.ShapeDtypeStruct((width, width), f32)),
        in_specs=[vmem, vmem],
        out_specs=(hbm, hbm),
        scratch_shapes=[dma((2,))],
    )(
        pltpu.with_memory_space_constraint(sketch, pltpu.VMEM),
        pltpu.with_memory_space_constraint(gram, pltpu.VMEM),
    )


def body(matrix, flip_bits, sample_rows):
    rows, width = matrix.shape
    n_grp, n_dev = lax.axis_size("grp"), lax.axis_size("dev")
    paired = sample_rows.shape[0] * 2 == n_grp * n_dev * LANES
    tiled = width == LANES and width % (n_grp * 16) == 0
    if paired and tiled and rows % LANES == 0:
        return plane_body(matrix, flip_bits, sample_rows)
    return general(matrix, flip_bits, sample_rows)


def solution(mesh):
    return jax.shard_map(
        body,
        mesh=mesh,
        in_specs=(P(("grp", "dev"), None), P(("grp", "dev")), P()),
        out_specs=(P(("grp", "dev"), None), P()),
        check_vma=False,
    )
```
